256 devices in a mesh: dp: 4 (over x), group: 4 (over y), member: 16 (over z, core).
Axes of the slice: x: 4, y: 4, z: 8, core: 2. Of those that a mesh axis runs over, the one named last changes fastest.
Arguments:
- tokens: bfloat16 [2048, 2880], P(('dp', 'group', 'member')), may hold values from -6 to 6
- cotangent: bfloat16 [2048, 2880], P(('dp', 'group', 'member')), may hold values from -6 to 6
- expert_ids: int32 [2048, 4], P(('dp', 'group', 'member')), may hold values from 0 to 7, all different within a row; in each aligned block of 8 rows (0 to 7, 8 to 15, ...) at most 8 rows name the same one
- gate_weights: float32 [2048, 4], P(('dp', 'group', 'member')), may hold values from 0.25 to 1
- w_gate: bfloat16 [8, 2880, 2880], P('group', 'member'), may hold values from -0.109375 to 0.109375
- w_up: bfloat16 [8, 2880, 2880], P('group', 'member'), may hold values from -0.109375 to 0.109375
- w_down: bfloat16 [8, 2880, 2880], P('group', 'member'), may hold values from -0.109375 to 0.109375
Outputs:
- grad_tokens: bfloat16 [2048, 2880], P(('dp', 'group', 'member'))
- grad_gate: bfloat16 [8, 2880, 2880], P('group', 'member', 'dp')
- grad_up: bfloat16 [8, 2880, 2880], P('group', 'member', 'dp')
- grad_down: bfloat16 [8, 2880, 2880], P('group', 'member', 'dp')
The draws below stay inside these ranges and needn't reach their ends.
Inputs may be any that keep to these rules, and one draw needn't show every extreme that they name: `expert_ids`: each row names 4 different experts. Among the rows of one device no expert is named by more than 8 rows, a bound that some block reaches of them.
All inputs are finite; a program needn't handle non-finite values.
Results may differ from the reference program's by a relative error of at most 0.02.
Values may be sent and summed in bfloat16 or wider, within the bound.
No kernel may reach another device: no remote copies, remote signals or barrier semaphores. Data moves between devices by JAX's collectives and lax.ppermute only.
A program may use at most 128 MiB of HBM per device.

```python
import math
import jax
import jax.numpy as jnp
import numpy as np
from jax import lax

D = 2880
HID = 2880
TOPK = 4
TOK_DEV = 8
EXPERTS = 8
CAP = 8
TOKENS = 2048
N_DP = 4


def level_of(own_key, shape, split, least, high):
    gain = 1.0
    for dim, shards_of in split:
        steps = jax.random.uniform(jax.random.fold_in(jax.random.fold_in(own_key, 6), dim), (shards_of,), jnp.float32, least / len(split), high / len(split))
        gain = gain * jnp.repeat(jnp.exp(steps), shape[dim] // shards_of).reshape((-1,) + (1,) * (len(shape) - 1 - dim))
    return gain


def routed_block(own_key, own, number, rows, amount, top, most, lean):
    order = jax.random.permutation(own_key, amount)
    packed, ordinary = load_shares(amount, rows * top, most, lean, True), load_shares(amount, rows * top, most, lean, False)
    places = jnp.arange(amount)

    def named(lengths, offset_by):
        used = int((lengths > 0).sum())
        fixed = max(1, used // 4)
        moved = fixed + (places - fixed + offset_by * (used - fixed)) % max(1, amount - fixed)
        return jnp.zeros((amount,), jnp.int32).at[order[jnp.where(places < fixed, places, moved)]].set(jnp.asarray(lengths, jnp.int32))

    lengths = jnp.where(number % 4 == 0, named(packed, number // 4), named(ordinary, number - number // 4 - 1))
    mixed = jax.random.permutation(jax.random.fold_in(own, 3), amount)
    source_of, taker = mixed[0:amount // 2 * 2:2], mixed[1:amount // 2 * 2:2]
    slack = jnp.minimum(lengths[source_of] - 1, most - lengths[taker]) // 2
    slack = jnp.where((source_of == order[0]) | (taker == order[0]) | (lengths[taker] == 0), 0, jnp.maximum(slack, 0))
    moved = jax.random.randint(jax.random.fold_in(own, 4), (amount // 2,), 0, 1 << 20) % (slack + 1)
    lengths = lengths.at[source_of].add(-moved).at[taker].add(moved)
    labels = jnp.searchsorted(jnp.cumsum(lengths), jnp.arange(rows * top), side="right").astype(jnp.int32)
    grid = labels.reshape(top, rows).T
    grid = grid[jax.random.permutation(jax.random.fold_in(own, 1), rows)]
    offset_by = jax.random.randint(jax.random.fold_in(own, 2), (rows, 1), 0, top)
    return jnp.take_along_axis(grid, (jnp.arange(top)[None, :] + offset_by) % top, axis=1)


def load_shares(amount, total, limit, lean, full):
    portions = [(1 << 20) // math.isqrt(grade ** lean) + 1 for grade in range(1, amount + 1)]
    largest = limit if full else min(limit, max(-(-total // amount), total * portions[0] // sum(portions)))
    least = 1 if total - largest >= amount - 1 else 0
    given, surplus = [largest] + [least] * (amount - 1), total - largest - least * (amount - 1)
    while surplus > 0:
        movable = [i for i in range(1, amount) if given[i] < largest] or [i for i in range(1, amount) if given[i] < limit]
        whole, left = sum([portions[i] for i in movable]), surplus
        for i in movable:
            extra = min(limit - given[i], max(1, left * portions[i] // whole), surplus)
            given[i] = given[i] + extra
            surplus = surplus - extra
    return np.array(given)


def scatter_about(rng, dims, scale, limit, cuts=(), held_as=jnp.bfloat16):
    result = scale * jax.random.normal(rng, dims, jnp.float32)
    if cuts:
        result = result * level_of(rng, dims, cuts, -0.22, 0.18)
    return jnp.clip(result, -limit, limit).astype(held_as)


def setup_inputs(seed: int = 0) -> dict:
    streams_of = jax.random.split(jax.random.key(seed), 8)
    tokens = scatter_about(streams_of[0], (TOKENS, D), 1.0, 6.0, ((0, 256),))
    cotangent = scatter_about(streams_of[1], (TOKENS, D), 1.0, 6.0, ((0, 256),))
    expert_ids_keys = jax.random.split(jax.random.fold_in(streams_of[2], 1), TOKENS // TOK_DEV)
    expert_ids_turns = jax.random.permutation(jax.random.fold_in(streams_of[2], 3), TOKENS // TOK_DEV)
    expert_ids = jax.vmap(lambda own, number: routed_block(jax.random.fold_in(streams_of[2], 2), own, number, TOK_DEV, EXPERTS, TOPK, CAP, 2))(expert_ids_keys, expert_ids_turns).reshape((TOKENS, TOPK))
    gate_weights = jnp.clip(0.25 + 0.75 * jax.random.uniform(streams_of[3], (TOKENS, TOPK), jnp.float32) ** level_of(streams_of[3], (TOKENS, TOPK), ((0, 256),), -0.2, 0.2), 0.25, 1.0)
    w_gate = scatter_about(streams_of[4], (EXPERTS, HID, D), D ** -0.5, 0.109375, ((0, 4), (1, 16)))
    w_up = scatter_about(streams_of[5], (EXPERTS, HID, D), D ** -0.5, 0.109375, ((0, 4), (1, 16)))
    w_down = scatter_about(streams_of[6], (EXPERTS, HID, D), HID ** -0.5, 0.109375, ((0, 4), (1, 16)))
    return dict(tokens=tokens, cotangent=cotangent, expert_ids=expert_ids, gate_weights=gate_weights, w_gate=w_gate, w_up=w_up, w_down=w_down)


def to_bf16(value):
    rounded = value.astype(jnp.bfloat16)
    rounded = lax.optimization_barrier(rounded)
    return rounded.astype(jnp.float32)


def reference(tokens, cotangent, expert_ids, gate_weights, w_gate, w_up, w_down):
    experts = w_gate.shape[0]
    token_count = tokens.shape[0]
    matches = expert_ids[:, :, None] == jnp.arange(experts, dtype=jnp.int32)[None, None, :]
    coefficient = jnp.sum(jnp.where(matches, gate_weights[:, :, None], 0.0), axis=1).astype(jnp.float32)
    inputs = tokens.astype(jnp.float32)
    upstream = cotangent.astype(jnp.float32)
    quarter = token_count // N_DP

    def expert_step(total, pieces):
        gate_mat, up_mat, down_mat, column = pieces
        gate_full = gate_mat.astype(jnp.float32)
        up_full = up_mat.astype(jnp.float32)
        down_full = down_mat.astype(jnp.float32)
        scaled = to_bf16(column[:, None] * upstream)
        gate_pre = jnp.dot(inputs, gate_full.T)
        up_pre = jnp.dot(inputs, up_full.T)
        sigmoid_gate = jax.nn.sigmoid(gate_pre)
        hidden = to_bf16(gate_pre * sigmoid_gate * up_pre)
        grad_hidden = jnp.dot(scaled, down_full.T)
        grad_up_pre = to_bf16(grad_hidden * gate_pre * sigmoid_gate)
        grad_gate_pre = to_bf16(grad_hidden * up_pre * sigmoid_gate * (1.0 + gate_pre * (1.0 - sigmoid_gate)))
        contribution = to_bf16(jnp.dot(grad_gate_pre, gate_full) + jnp.dot(grad_up_pre, up_full))
        total = total + contribution
        split_inputs = inputs.reshape(N_DP, quarter, -1)
        split_gate = grad_gate_pre.reshape(N_DP, quarter, -1)
        split_up = grad_up_pre.reshape(N_DP, quarter, -1)
        split_hidden = hidden.reshape(N_DP, quarter, -1)
        split_scaled = scaled.reshape(N_DP, quarter, -1)
        grad_gate = jnp.sum(to_bf16(jnp.einsum("qth,qtd->qhd", split_gate, split_inputs)), axis=0)
        grad_up = jnp.sum(to_bf16(jnp.einsum("qth,qtd->qhd", split_up, split_inputs)), axis=0)
        grad_down = jnp.sum(to_bf16(jnp.einsum("qth,qtd->qhd", split_hidden, split_scaled)), axis=0)
        return total, (grad_gate.astype(jnp.bfloat16), grad_up.astype(jnp.bfloat16), grad_down.astype(jnp.bfloat16))

    start_total = jnp.zeros(tokens.shape, jnp.float32)
    total, grads = lax.scan(expert_step, start_total, (w_gate, w_up, w_down, coefficient.T))
    return total.astype(jnp.bfloat16), grads[0], grads[1], grads[2]
```

```python
import jax
import jax.numpy as jnp
from jax import lax
from jax.experimental import pallas as pl
from jax.experimental.pallas import tpu as pltpu
from jax.sharding import PartitionSpec as P

LANE = 128
SUB = 16


def up_to(n, k):
    return -(-n // k) * k


def whole(*shape):
    return pl.BlockSpec(shape, lambda *_: (0,) * len(shape))


def pack_weights(w_gate, w_up, w_down):
    n_exp, hid, width = w_gate.shape
    pad = up_to(hid, SUB * 4)

    def kernel(g_ref, u_ref, d_ref, cat_ref, down_ref):
        cat_ref[...] = jnp.zeros_like(cat_ref)
        down_ref[...] = jnp.zeros_like(down_ref)
        for e in range(n_exp):
            cat_ref[e * pad : e * pad + hid, :] = g_ref[e]
            cat_ref[(n_exp + e) * pad : (n_exp + e) * pad + hid, :] = u_ref[e]
            down_ref[e * pad : e * pad + hid, :] = d_ref[e]

    return pl.pallas_call(
        kernel,
        out_shape=(
            jax.ShapeDtypeStruct((2 * n_exp * pad, width), jnp.bfloat16),
            jax.ShapeDtypeStruct((n_exp * pad, width), jnp.bfloat16),
        ),
        name="pack_weights",
    )(w_gate, w_up, w_down)


def forward(own, far, first, cat, down, width, n_exp, n_near, n_group):
    _, half, padded = own.shape
    span = down.shape[0]
    pad = span // n_exp
    tall = 2 * half
    rows = half // n_near
    bf = jnp.bfloat16
    nt = (((1,), (1,)), ((), ()))

    def kernel(first_ref, own_ref, far_ref, cat_ref, down_ref, act_ref, near_ref, away_ref):
        x = jnp.concatenate([own_ref[0, :, :width], far_ref[0, :, :width]], axis=0)
        y = jnp.concatenate([own_ref[1, :, :width], far_ref[1, :, :width]], axis=0)
        pre = lax.dot_general(x, cat_ref[...], nt, preferred_element_type=jnp.float32)
        back = lax.dot_general(y, down_ref[...], nt, preferred_element_type=jnp.float32)
        gate = pre[:, :span]
        up = pre[:, span:]
        tail = jnp.concatenate(
            [own_ref[0, :, width:].astype(jnp.float32), far_ref[0, :, width:].astype(jnp.float32)], axis=0
        )
        lanes = lax.broadcasted_iota(jnp.int32, tail.shape, 1)
        experts = tail.shape[1] // 4
        column = lax.broadcasted_iota(jnp.int32, gate.shape, 1)
        coef = jnp.zeros_like(gate)
        for e in range(n_exp):
            wanted = first_ref[0] + e
            hit = (lanes == wanted) | (lanes == wanted + experts)
            mine = jnp.sum(jnp.where(hit, tail, 0.0), axis=1, keepdims=True)
            coef = jnp.where((column >= e * pad) & (column < (e + 1) * pad), mine, coef)
        sig = jax.nn.sigmoid(gate)
        silu = gate * sig
        back = back * coef
        act_ref[:, :span] = (back * up * sig * (1.0 + gate * (1.0 - sig))).astype(bf)
        act_ref[:, span : 2 * span] = (back * silu).astype(bf)
        act_ref[:, 2 * span :] = (coef * (silu * up)).astype(bf)
        part = jnp.dot(act_ref[:, : 2 * span], cat_ref[...], preferred_element_type=jnp.float32).astype(bf)
        span_rows = near_ref.shape[2]
        for c, ref in enumerate((near_ref, away_ref)):
            for z in range(n_near):
                for g in range(ref.shape[0]):
                    at = c * half + z * rows + g * span_rows
                    ref[g, z] = part[at : at + span_rows]

    groups = n_group
    sums = jax.ShapeDtypeStruct((groups, n_near, rows // groups, width), bf)
    return pl.pallas_call(
        kernel,
        out_shape=(jax.ShapeDtypeStruct((tall, 3 * span), bf), sums, sums),
        in_specs=[pl.BlockSpec(memory_space=pltpu.SMEM)] + [pl.BlockSpec(memory_space=pltpu.VMEM)] * 4,
        out_specs=(pl.BlockSpec(memory_space=pltpu.VMEM),) * 3,
        cost_estimate=pl.CostEstimate(
            flops=2 * tall * width * 5 * span, bytes_accessed=16 << 20, transcendentals=tall * span
        ),
        name="forward",
    )(first, own, far, cat, down)


def weight_sums(act, own, far, total, hid, n_exp, n_dp):
    _, half, width = own.shape
    span = act.shape[-1] // 3
    pad = span // n_exp
    cols = width // n_dp
    tall = n_dp * 2 * half
    tn = (((0,), (0,)), ((), ()))
    last = total is not None
    kind_of = jnp.bfloat16 if last else jnp.float32

    def kernel(*refs):
        act_ref, own_ref, far_ref = refs[:3]
        total_ref = refs[3] if last else None
        outs = refs[-5:-2] if last else refs[-3:-2]
        x_ref, y_ref = refs[-2:]
        for p in range(n_dp):
            for c, ref in enumerate((own_ref, far_ref)):
                at = (2 * p + c) * half
                x_ref[at : at + half, :] = ref[0, :, p * cols : (p + 1) * cols]
                y_ref[at : at + half, :] = ref[1, :, p * cols : (p + 1) * cols]
        for kind in range(3):
            part = lax.dot_general(
                act_ref[:, kind * span : (kind + 1) * span],
                (y_ref if kind == 2 else x_ref)[...],
                tn,
                preferred_element_type=jnp.float32,
            )
            for e in range(n_exp):
                mine = part[e * pad : e * pad + hid, :]
                if last:
                    outs[kind][e] = (mine + total_ref[kind * n_exp + e]).astype(jnp.bfloat16)
                else:
                    outs[0][kind * n_exp + e] = mine

    if last:
        shape = (jax.ShapeDtypeStruct((n_exp, hid, cols), jnp.bfloat16),) * 3
    else:
        shape = (jax.ShapeDtypeStruct((3 * n_exp, hid, cols), jnp.float32),)
    operands = (act.reshape(tall, 3 * span), own, far) + ((total,) if last else ())
    return pl.pallas_call(
        kernel,
        out_shape=shape,
        in_specs=[pl.BlockSpec(memory_space=pltpu.VMEM)] * len(operands),
        out_specs=(pl.BlockSpec(memory_space=pltpu.VMEM),) * len(shape),
        scratch_shapes=[pltpu.VMEM((tall, cols), jnp.bfloat16)] * 2,
        cost_estimate=pl.CostEstimate(
            flops=2 * tall * 3 * span * cols, bytes_accessed=12 << 20, transcendentals=0
        ),
        name="weight_sums",
    )(*operands)


def shifted(x, axis, step, n):
    return lax.ppermute(x, axis, [(i, (i - step) % n) for i in range(n)])


def group_gather(x):
    n = lax.axis_size("group")
    return jnp.concatenate([x] + [shifted(x, "group", k, n) for k in range(1, n)], axis=1)


def ring(x):
    n = lax.axis_size("member")
    half = x.shape[1] // 2
    lo, hi = [x], [x]
    for _ in range(3):
        lo.append(shifted(lo[-1], "member", -2, n))
        hi.append(shifted(hi[-1], "member", 2, n))
    top = shifted(lo[3][:, :half], "member", -2, n)
    bottom = shifted(hi[3][:, half:], "member", 2, n)
    first = jnp.concatenate([x, lo[1], hi[1], lo[2], hi[2]], axis=1)
    second = jnp.concatenate([lo[3], hi[3], top, bottom], axis=1)
    return first, second


OFFSETS = (0, -1, 1, -2, 2, -3, 3, 4)


def partner(x):
    n = lax.axis_size("member")
    return lax.ppermute(x, "member", [(i, i ^ 1) for i in range(n)])


def to_planes(act):
    n_dp = lax.axis_size("dp")
    return lax.all_to_all(jnp.broadcast_to(act[None], (n_dp,) + act.shape), "dp", split_axis=0, concat_axis=0, tiled=True)


def on_device(tokens, cotangent, expert_ids, gate_weights, w_gate, w_up, w_down):
    n_group = lax.axis_size("group")
    n_member = lax.axis_size("member")
    n_dp = lax.axis_size("dp")
    n_exp, hid, width = w_gate.shape
    experts = n_exp * n_group
    rows = tokens.shape[0]
    cols = width // n_dp
    padded = up_to(width, LANE)
    room = padded - width
    bf = jnp.bfloat16
    matches = expert_ids[:, :, None] == jnp.arange(experts, dtype=jnp.int32)[None, None, :]
    coefficient = jnp.sum(jnp.where(matches, gate_weights[:, :, None], 0.0), axis=1)
    high = coefficient.astype(bf)
    low = (coefficient - high.astype(jnp.float32)).astype(bf)
    quarter = room // 4
    tail = jnp.concatenate(
        [
            jnp.pad(high, ((0, 0), (0, quarter - experts))),
            jnp.pad(low, ((0, 0), (0, room - quarter - experts))),
        ],
        axis=1,
    )
    rows_in = jnp.stack(
        [
            jnp.concatenate([tokens, tail], axis=1),
            jnp.pad(cotangent, ((0, 0), (0, room))),
        ]
    )
    first_rows, second_rows = ring(group_gather(rows_in))
    both = jnp.stack([tokens, cotangent]).reshape(2 * rows, n_dp, cols)
    cut = lax.all_to_all(both.transpose(1, 0, 2), "dp", split_axis=0, concat_axis=0, tiled=True)
    cut = cut.transpose(1, 0, 2).reshape(2, rows, width)
    first_cut, second_cut = ring(group_gather(cut))
    cat, down = pack_weights(w_gate, w_up, w_down)
    first = (lax.axis_index("group") * n_exp).astype(jnp.int32).reshape(1)
    act_1, near_1, away_1 = forward(first_rows, partner(first_rows), first, cat, down, width, n_exp, 5, n_group)
    act_2, near_2, away_2 = forward(second_rows, partner(second_rows), first, cat, down, width, n_exp, 3, n_group)
    planes_1 = to_planes(act_1)
    planes_2 = to_planes(act_2)
    total = weight_sums(planes_1, first_cut, partner(first_cut), None, hid, n_exp, n_dp)[0]
    grads = weight_sums(planes_2, second_cut, partner(second_cut), total, hid, n_exp, n_dp)

    def over_groups(near, away):
        f32 = jnp.float32
        mine = (near.astype(f32) + partner(away).astype(f32)).astype(bf)
        total = mine[0].astype(f32)
        for k in range(1, n_group):
            total = total + shifted(mine[k], "group", -k, n_group).astype(f32)
        return total.astype(bf)

    reduced = jnp.concatenate([over_groups(near_1, away_1), over_groups(near_2, away_2)], axis=0)
    chips = n_member // 2
    at = lax.axis_index("member") // 2
    order = (jnp.arange(chips) - at + 3) % chips
    place = jnp.asarray([OFFSETS.index(k - 3) for k in range(chips)], jnp.int32)[order]
    hot = (place[:, None] == jnp.arange(chips)[None, :]).astype(bf)
    sorted_rows = jnp.dot(hot, reduced.reshape(chips, rows * width), preferred_element_type=jnp.float32).astype(bf)
    peers = [[2 * i + c for i in range(chips)] for c in range(2)]
    back = lax.all_to_all(
        sorted_rows.reshape(chips, rows, width), "member", split_axis=0, concat_axis=0, axis_index_groups=peers, tiled=True
    )
    grad_tokens = jnp.sum(back.astype(jnp.float32), axis=0).astype(bf)
    return (grad_tokens,) + tuple(grads)


def solution(mesh):
    placed = P(("dp", "group", "member"), None)
    weight = P("group", "member", None)
    grad = P("group", "member", "dp")
    return jax.shard_map(
        on_device,
        mesh=mesh,
        in_specs=(placed, placed, placed, placed, weight, weight, weight),
        out_specs=(placed, grad, grad, grad),
        check_vma=False,
    )
```

```python
import jax
import jax.numpy as jnp
from jax import lax
from jax.experimental import pallas as pl
from jax.experimental.pallas import tpu as pltpu
from jax.sharding import PartitionSpec as P

LANE = 128
PAD = 64
MIB = 1 << 20
OFFSETS = (0, -1, 1, -2, 2, -3, 3, 4)
VMEM = pl.BlockSpec(memory_space=pltpu.VMEM)
SMEM = pl.BlockSpec(memory_space=pltpu.SMEM)


def up_to(n, k):
    return -(-n // k) * k


def prepare(tokens, cotangent, expert_ids, gate_weights, experts, padded):
    rows, width = tokens.shape
    room = padded - width
    quarter = room // 4
    bf = jnp.bfloat16

    def kernel(tok_ref, cot_ref, id_ref, weight_ref, out_ref):
        lane = lax.broadcasted_iota(jnp.int32, (rows, room), 1)
        expert = jnp.where(lane < quarter, lane, lane - quarter)
        coef = jnp.zeros((rows, room), jnp.float32)
        for k in range(id_ref.shape[1]):
            coef = coef + jnp.where(id_ref[:, k : k + 1] == expert, weight_ref[:, k : k + 1], 0.0)
        high = coef.astype(bf).astype(jnp.float32)
        tail = jnp.where(lane < quarter, high, jnp.where(lane < 2 * quarter, coef - high, 0.0))
        out_ref[0, :, :width] = tok_ref[...]
        out_ref[0, :, width:] = tail.astype(bf)
        out_ref[1, :, :width] = cot_ref[...]
        out_ref[1, :, width:] = jnp.zeros((rows, room), bf)

    return pl.pallas_call(
        kernel,
        out_shape=jax.ShapeDtypeStruct((2, rows, padded), bf),
        compiler_params=pltpu.CompilerParams(vmem_limit_bytes=4 * MIB),
        name="prepare",
    )(tokens, cotangent, expert_ids, gate_weights)


def join(pieces):
    lead, rows, width = pieces[0].shape

    def kernel(*refs):
        for i, ref in enumerate(refs[:-1]):
            refs[-1][:, i * rows : (i + 1) * rows, :] = ref[...]

    return pl.pallas_call(
        kernel,
        out_shape=jax.ShapeDtypeStruct((lead, rows * len(pieces), width), pieces[0].dtype),
        compiler_params=pltpu.CompilerParams(vmem_limit_bytes=4 * MIB),
        name="join",
    )(*pieces)


def pack_weights(w_gate, w_up, w_down):
    n_exp, hid, width = w_gate.shape
    pad = up_to(hid, PAD)

    def kernel(g_ref, u_ref, d_ref, cat_ref, down_ref):
        zero = jnp.zeros((pad - hid, cat_ref.shape[1]), jnp.bfloat16)
        for ref, out_ref, base in ((g_ref, cat_ref, 0), (u_ref, cat_ref, n_exp), (d_ref, down_ref, 0)):
            for e in range(n_exp):
                at = (base + e) * pad
                out_ref[at : at + hid, :] = ref[:, e, :]
                out_ref[at + hid : at + pad, :] = zero

    cols = 5 * LANE
    steps = pl.cdiv(width, cols)
    by_cols = lambda i: (0, i)
    stored = pl.BlockSpec((hid, n_exp, cols), lambda i: (0, 0, i))
    return pl.pallas_call(
        kernel,
        grid=(steps,),
        out_shape=(
            jax.ShapeDtypeStruct((2 * n_exp * pad, width), jnp.bfloat16),
            jax.ShapeDtypeStruct((n_exp * pad, width), jnp.bfloat16),
        ),
        in_specs=[stored] * 3,
        out_specs=(pl.BlockSpec((2 * n_exp * pad, cols), by_cols), pl.BlockSpec((n_exp * pad, cols), by_cols)),
        compiler_params=pltpu.CompilerParams(vmem_limit_bytes=10 * MIB),
        name="pack_weights",
    )(*(w.transpose(1, 0, 2) for w in (w_gate, w_up, w_down)))


def forward(own, far, first, cat, down, width, n_exp, n_group, n_dp):
    half = sum(p.shape[1] for p in own)
    tall = 2 * half
    span = down.shape[0]
    pad = span // n_exp
    cols = width // n_dp
    bf = jnp.bfloat16
    f32 = jnp.float32
    nt = (((1,), (1,)), ((), ()))
    pieces = tuple(own) + tuple(far)
    block = 8 * n_group
    n_near = half // block

    def kernel(first_ref, *refs):
        rows = refs[: len(pieces)]
        cat_ref, down_ref, act_ref, near_ref, away_ref, cut_ref = refs[len(pieces) :]
        x = jnp.concatenate([r[0, :, :width] for r in rows], axis=0)
        y = jnp.concatenate([r[1, :, :width] for r in rows], axis=0)
        pre = lax.dot_general(x, cat_ref[...], nt, preferred_element_type=f32)
        back = lax.dot_general(y, down_ref[...], nt, preferred_element_type=f32)
        for d in range(n_dp):
            cut_ref[0, d] = x[:, d * cols : (d + 1) * cols]
            cut_ref[1, d] = y[:, d * cols : (d + 1) * cols]
        gate = pre[:, :span]
        up = pre[:, span:]
        tail = jnp.concatenate([r[0, :, width:] for r in rows], axis=0).astype(f32)
        lanes = lax.broadcasted_iota(jnp.int32, tail.shape, 1)
        quarter = tail.shape[1] // 4
        column = lax.broadcasted_iota(jnp.int32, gate.shape, 1)
        coef = jnp.zeros_like(gate)
        for e in range(n_exp):
            wanted = first_ref[0] + e
            hit = (lanes == wanted) | (lanes == wanted + quarter)
            mine = jnp.sum(jnp.where(hit, tail, 0.0), axis=1, keepdims=True)
            coef = jnp.where((column >= e * pad) & (column < (e + 1) * pad), mine, coef)
        sig = jax.nn.sigmoid(gate)
        silu = gate * sig
        back = back * coef
        act_ref[:, :span] = (back * up * sig * (1.0 + gate * (1.0 - sig))).astype(bf)
        act_ref[:, span : 2 * span] = (back * silu).astype(bf)
        act_ref[:, 2 * span :] = (coef * (silu * up)).astype(bf)
        part = jnp.dot(act_ref[:, : 2 * span], cat_ref[...], preferred_element_type=f32).astype(bf)
        for c, ref in enumerate((near_ref, away_ref)):
            for z in range(n_near):
                for g in range(n_group):
                    at = c * half + z * block + g * 8
                    ref[g, z] = part[at : at + 8]

    sums = jax.ShapeDtypeStruct((n_group, n_near, 8, width), bf)
    return pl.pallas_call(
        kernel,
        out_shape=(
            jax.ShapeDtypeStruct((tall, 3 * span), bf),
            sums,
            sums,
            jax.ShapeDtypeStruct((2, n_dp, tall, cols), bf),
        ),
        in_specs=[SMEM] + [VMEM] * (len(pieces) + 2),
        out_specs=(VMEM,) * 4,
        compiler_params=pltpu.CompilerParams(vmem_limit_bytes=12 * MIB),
        cost_estimate=pl.CostEstimate(
            flops=2 * tall * width * 5 * span, bytes_accessed=12 * MIB, transcendentals=tall * span
        ),
        name="forward",
    )(first, *pieces, cat, down)


def column_sums(which, act_1, act_2, cut_1, cut_2, hid, n_exp):
    span = act_1.shape[1] // 3
    pad = span // n_exp
    cols = cut_1.shape[-1]
    tn = (((0,), (0,)), ((), ()))

    def kernel(which_ref, a_ref, b_ref, c_ref, d_ref, *outs):
        del which_ref
        act = jnp.concatenate([a_ref[...], b_ref[...]], axis=0)
        for kind in range(3):
            side = kind // 2
            x = jnp.concatenate([c_ref[side, 0], d_ref[side, 0]], axis=0)
            part = lax.dot_general(
                act[:, kind * span : (kind + 1) * span], x, tn, preferred_element_type=jnp.float32
            ).astype(jnp.bfloat16)
            for e in range(n_exp):
                outs[e][kind] = part[e * pad : e * pad + hid, :]

    fixed = lambda n: (lambda i, w: (0,) * n)
    picked = lambda i, w: (0, w[0], 0, 0)
    return pl.pallas_call(
        kernel,
        out_shape=(jax.ShapeDtypeStruct((3, hid, cols), jnp.bfloat16),) * n_exp,
        grid_spec=pltpu.PrefetchScalarGridSpec(
            num_scalar_prefetch=1,
            grid=(1,),
            in_specs=[
                pl.BlockSpec(act_1.shape, fixed(2)),
                pl.BlockSpec(act_2.shape, fixed(2)),
                pl.BlockSpec((2, 1) + cut_1.shape[2:], picked),
                pl.BlockSpec((2, 1) + cut_2.shape[2:], picked),
            ],
            out_specs=(pl.BlockSpec((3, hid, cols), fixed(3)),) * n_exp,
        ),
        compiler_params=pltpu.CompilerParams(vmem_limit_bytes=8 * MIB),
        cost_estimate=pl.CostEstimate(
            flops=2 * 512 * 3 * span * cols, bytes_accessed=4 * MIB, transcendentals=0
        ),
        name="column_sums",
    )(which, act_1, act_2, cut_1, cut_2)


def finish(parts):
    n_exp = len(parts)
    _, hid, cols = parts[0][0].shape

    def kernel(*refs):
        outs = refs[-3:]
        at = 0
        for e in range(n_exp):
            mine = refs[at : at + len(parts[e])]
            at += len(parts[e])
            for kind in range(3):
                total = mine[0][kind].astype(jnp.float32)
                for r in mine[1:]:
                    total = total + r[kind].astype(jnp.float32)
                outs[kind][:, e, :] = total.astype(jnp.bfloat16)

    flat = [a for p in parts for a in p]
    outs = pl.pallas_call(
        kernel,
        grid=(1,),
        out_shape=(jax.ShapeDtypeStruct((hid, n_exp, cols), jnp.bfloat16),) * 3,
        in_specs=[pl.BlockSpec(a.shape, lambda i: (0, 0, 0)) for a in flat],
        out_specs=(pl.BlockSpec((hid, n_exp, cols), lambda i: (0, 0, 0)),) * 3,
        compiler_params=pltpu.CompilerParams(vmem_limit_bytes=12 * MIB),
        name="finish",
    )(*flat)
    return tuple(o.transpose(1, 0, 2) for o in outs)


def small(kernel, out_shape, operands, name, scalars=0):
    return pl.pallas_call(
        kernel,
        out_shape=out_shape,
        in_specs=[SMEM] * scalars + [VMEM] * (len(operands) - scalars),
        out_specs=jax.tree.map(lambda _: VMEM, out_shape),
        compiler_params=pltpu.CompilerParams(vmem_limit_bytes=4 * MIB),
        name=name,
    )(*operands)


def halves(lo, hi):
    lead, rows, width = lo.shape
    half = rows // 2

    def kernel(lo_ref, hi_ref, top_ref, bottom_ref):
        top_ref[...] = lo_ref[:, :half, :]
        bottom_ref[...] = hi_ref[:, half:, :]

    piece = jax.ShapeDtypeStruct((lead, half, width), lo.dtype)
    return small(kernel, (piece, piece), (lo, hi), "halves")


def add(a, b):
    def kernel(a_ref, b_ref, out_ref):
        for k in range(a.shape[0]):
            out_ref[k] = (a_ref[k].astype(jnp.float32) + b_ref[k].astype(jnp.float32)).astype(a.dtype)

    return small(kernel, jax.ShapeDtypeStruct(a.shape, a.dtype), (a, b), "add")


def merge_cores(near, arrived):
    n_group = near.shape[0]

    def kernel(a_ref, b_ref, *outs):
        for k in range(n_group):
            outs[k][...] = (a_ref[k].astype(jnp.float32) + b_ref[k].astype(jnp.float32)).astype(jnp.bfloat16)

    one = jax.ShapeDtypeStruct(near.shape[1:], near.dtype)
    return small(kernel, (one,) * n_group, (near, arrived), "merge_cores")


def by_chip(at, first, second, chips):
    count = len(first)
    shape = first[0].shape[1:]

    def kernel(at_ref, *refs):
        out_ref = refs[-1]
        here = at_ref[0]
        for j, offset in enumerate(OFFSETS):
            mine, k = (refs[:count], j) if j < first[0].shape[0] else (refs[count : 2 * count], j - first[0].shape[0])
            total = mine[0][k].astype(jnp.float32)
            for r in mine[1:]:
                total = total + r[k].astype(jnp.float32)
            out_ref[lax.rem(here + (offset + chips), chips)] = total.astype(jnp.bfloat16)

    out = jax.ShapeDtypeStruct((chips,) + shape, jnp.bfloat16)
    return small(kernel, out, (at, *first, *second), "by_chip", 1)


def total_of(parts):
    def kernel(in_ref, out_ref):
        total = in_ref[0].astype(jnp.float32)
        for k in range(1, parts.shape[0]):
            total = total + in_ref[k].astype(jnp.float32)
        out_ref[...] = total.astype(jnp.bfloat16)

    return small(kernel, jax.ShapeDtypeStruct(parts.shape[1:], jnp.bfloat16), (parts,), "total_of")


def shifted(x, axis, step):
    n = lax.axis_size(axis)
    return lax.ppermute(x, axis, [(i, (i - step) % n) for i in range(n)])


def partner(x):
    n = lax.axis_size("member")
    return lax.ppermute(x, "member", [(i, i ^ 1) for i in range(n)])


def on_device(tokens, cotangent, expert_ids, gate_weights, w_gate, w_up, w_down):
    n_group = lax.axis_size("group")
    n_member = lax.axis_size("member")
    n_dp = lax.axis_size("dp")
    n_exp, hid, width = w_gate.shape
    rows = tokens.shape[0]
    padded = up_to(width, LANE)
    mine = prepare(tokens, cotangent, expert_ids, gate_weights, n_exp * n_group, padded)
    own = join([mine] + [shifted(mine, "group", k) for k in range(1, n_group)])
    lo, hi, lo_far, hi_far = [own], [own], [], []
    own_far = partner(own)
    cat, down = pack_weights(w_gate, w_up, w_down)
    for step in range(3):
        lo.append(shifted(lo[-1], "member", -2))
        hi.append(shifted(hi[-1], "member", 2))
        if step == 0:
            lo[-1], hi[-1], cat, down = lax.optimization_barrier((lo[-1], hi[-1], cat, down))
        lo_far.append(partner(lo[-1]))
        hi_far.append(partner(hi[-1]))
    top, bottom = halves(lo[3], hi[3])
    top = shifted(top, "member", -2)
    bottom = shifted(bottom, "member", 2)
    first = (lax.axis_index("group") * n_exp).astype(jnp.int32).reshape(1)
    act_1, near_1, away_1, cut_1 = forward(
        [own, lo[1], hi[1], lo[2], hi[2]],
        [own_far, lo_far[0], hi_far[0], lo_far[1], hi_far[1]],
        first, cat, down, width, n_exp, n_group, n_dp,
    )
    top, bottom, act_1 = lax.optimization_barrier((top, bottom, act_1))
    act_2, near_2, away_2, cut_2 = forward(
        [lo[3], hi[3], top, bottom],
        [lo_far[2], hi_far[2], partner(top), partner(bottom)],
        first, cat, down, width, n_exp, n_group, n_dp,
    )
    place = lax.axis_index("dp")

    def share(k):
        which = ((place + k) % n_dp).astype(jnp.int32).reshape(1)
        return column_sums(which, act_1, act_2, cut_1, cut_2, hid, n_exp)

    far_0, far_1 = share(2)
    right_0 = shifted(far_0, "dp", -1)
    left_1 = shifted(far_1, "dp", 1)
    next_0, next_1 = share(1)
    prev_0, prev_1 = share(3)
    from_left_1 = shifted(next_1, "dp", -1)
    from_right_0 = shifted(prev_0, "dp", 1)
    here_0, here_1 = share(0)
    from_left_0 = shifted(add(next_0, right_0), "dp", -1)
    from_right_1 = shifted(add(prev_1, left_1), "dp", 1)
    grads = finish([[here_0, from_right_0, from_left_0], [here_1, from_left_1, from_right_1]])

    def over_groups(near, away):
        both = merge_cores(near, partner(away))
        return [both[0]] + [shifted(both[k], "group", -k) for k in range(1, n_group)]

    chips = n_member // 2
    at = (lax.axis_index("member") // 2).astype(jnp.int32).reshape(1)
    sorted_rows = by_chip(at, over_groups(near_1, away_1), over_groups(near_2, away_2), chips)
    peers = [[2 * i + c for i in range(chips)] for c in range(2)]
    back = lax.all_to_all(
        sorted_rows, "member", split_axis=0, concat_axis=0, axis_index_groups=peers, tiled=True
    )
    grad_tokens = total_of(back)
    return (grad_tokens,) + tuple(grads)


def solution(mesh):
    placed = P(("dp", "group", "member"), None)
    weight = P("group", "member", None)
    grad = P("group", "member", "dp")
    return jax.shard_map(
        on_device,
        mesh=mesh,
        in_specs=(placed, placed, placed, placed, weight, weight, weight),
        out_specs=(placed, grad, grad, grad),
        check_vma=False,
    )
```

```python
import jax
import jax.numpy as jnp
from jax import lax
from jax.experimental import pallas as pl
from jax.experimental.pallas import tpu as pltpu
from jax.sharding import PartitionSpec as P

LANE = 128
PAD = 64
MIB = 1 << 20
OFFSETS = (0, -1, 1, -2, 2, -3, 3, 4)
VMEM = pl.BlockSpec(memory_space=pltpu.VMEM)
SMEM = pl.BlockSpec(memory_space=pltpu.SMEM)


def up_to(n, k):
    return -(-n // k) * k


def prepare(tokens, cotangent, expert_ids, gate_weights, experts, padded):
    rows, width = tokens.shape
    room = padded - width
    quarter = room // 4
    bf = jnp.bfloat16

    def kernel(tok_ref, cot_ref, id_ref, weight_ref, out_ref):
        lane = lax.broadcasted_iota(jnp.int32, (rows, room), 1)
        expert = jnp.where(lane < quarter, lane, lane - quarter)
        diagonal = lax.broadcasted_iota(jnp.int32, (rows, rows), 0) == lax.broadcasted_iota(jnp.int32, (rows, rows), 1)
        coef = jnp.zeros((rows, room), jnp.float32)
        for k in range(id_ref.shape[0]):
            ids = jnp.sum(jnp.where(diagonal, id_ref[k : k + 1, :], 0), axis=1, keepdims=True)
            weights = jnp.sum(jnp.where(diagonal, weight_ref[k : k + 1, :], 0.0), axis=1, keepdims=True)
            coef = coef + jnp.where(ids == expert, weights, 0.0)
        high = coef.astype(bf).astype(jnp.float32)
        tail = jnp.where(lane < quarter, high, jnp.where(lane < 2 * quarter, coef - high, 0.0))
        out_ref[0, :, :width] = tok_ref[...]
        out_ref[0, :, width:] = tail.astype(bf)
        out_ref[1, :, :width] = cot_ref[...]
        out_ref[1, :, width:] = jnp.zeros((rows, room), bf)

    operands = (tokens, cotangent, expert_ids.T, gate_weights.T)
    return pl.pallas_call(
        kernel,
        grid=(1,),
        out_shape=jax.ShapeDtypeStruct((2, rows, padded), bf),
        in_specs=[pl.BlockSpec(x.shape, lambda i: (0, 0)) for x in operands],
        out_specs=VMEM,
        compiler_params=pltpu.CompilerParams(vmem_limit_bytes=4 * MIB),
        name="prepare",
    )(*operands)


def join(pieces):
    lead, rows, width = pieces[0].shape

    def kernel(*refs):
        for i, ref in enumerate(refs[:-1]):
            refs[-1][:, i * rows : (i + 1) * rows, :] = ref[...]

    return pl.pallas_call(
        kernel,
        out_shape=jax.ShapeDtypeStruct((lead, rows * len(pieces), width), pieces[0].dtype),
        compiler_params=pltpu.CompilerParams(vmem_limit_bytes=4 * MIB),
        name="join",
    )(*pieces)


def pack_weights(w_gate, w_up, w_down):
    n_exp, hid, width = w_gate.shape
    pad = up_to(hid, PAD)

    def kernel(g_ref, u_ref, d_ref, cat_ref, down_ref):
        i = pl.program_id(0)
        zero = jnp.zeros((pad - hid, width), jnp.bfloat16)
        cat_ref[hid:, :] = zero
        down_ref[hid:, :] = zero
        down_ref[:hid, :] = d_ref[0]

        @pl.when(i < n_exp)
        def _():
            cat_ref[:hid, :] = g_ref[0]

        @pl.when(i >= n_exp)
        def _():
            cat_ref[:hid, :] = u_ref[0]

    return pl.pallas_call(
        kernel,
        grid=(2 * n_exp,),
        out_shape=(
            jax.ShapeDtypeStruct((2 * n_exp * pad, width), jnp.bfloat16),
            jax.ShapeDtypeStruct((n_exp * pad, width), jnp.bfloat16),
        ),
        in_specs=[
            pl.BlockSpec((1, hid, width), lambda i: (jnp.minimum(i, n_exp - 1), 0, 0)),
            pl.BlockSpec((1, hid, width), lambda i: (jnp.maximum(i - n_exp, 0), 0, 0)),
            pl.BlockSpec((1, hid, width), lambda i: (i // 2, 0, 0)),
        ],
        out_specs=(
            pl.BlockSpec((pad, width), lambda i: (i, 0)),
            pl.BlockSpec((pad, width), lambda i: (i // 2, 0)),
        ),
        compiler_params=pltpu.CompilerParams(vmem_limit_bytes=14 * MIB),
        name="pack_weights",
    )(w_gate, w_up, w_down)


def forward(own, far, first, cat, down, width, n_exp, n_group, n_dp):
    half = sum(p.shape[1] for p in own)
    tall = 2 * half
    span = down.shape[0]
    pad = span // n_exp
    cols = width // n_dp
    bf = jnp.bfloat16
    f32 = jnp.float32
    nt = (((1,), (1,)), ((), ()))
    pieces = tuple(own) + tuple(far)
    block = 8 * n_group
    n_near = half // block

    def kernel(first_ref, *refs):
        rows = refs[: len(pieces)]
        cat_ref, down_ref, act_ref, near_ref, away_ref, cut_ref = refs[len(pieces) :]
        x = jnp.concatenate([r[0, :, :width] for r in rows], axis=0)
        y = jnp.concatenate([r[1, :, :width] for r in rows], axis=0)
        pre = lax.dot_general(x, cat_ref[...], nt, preferred_element_type=f32)
        back = lax.dot_general(y, down_ref[...], nt, preferred_element_type=f32)
        for d in range(n_dp):
            cut_ref[0, d] = x[:, d * cols : (d + 1) * cols]
            cut_ref[1, d] = y[:, d * cols : (d + 1) * cols]
        gate = pre[:, :span]
        up = pre[:, span:]
        tail = jnp.concatenate([r[0, :, width:] for r in rows], axis=0).astype(f32)
        lanes = lax.broadcasted_iota(jnp.int32, tail.shape, 1)
        quarter = tail.shape[1] // 4
        column = lax.broadcasted_iota(jnp.int32, gate.shape, 1)
        coef = jnp.zeros_like(gate)
        for e in range(n_exp):
            wanted = first_ref[0] + e
            hit = (lanes == wanted) | (lanes == wanted + quarter)
            mine = jnp.sum(jnp.where(hit, tail, 0.0), axis=1, keepdims=True)
            coef = jnp.where((column >= e * pad) & (column < (e + 1) * pad), mine, coef)
        sig = jax.nn.sigmoid(gate)
        silu = gate * sig
        back = back * coef
        act_ref[:, :span] = (back * up * sig * (1.0 + gate * (1.0 - sig))).astype(bf)
        act_ref[:, span : 2 * span] = (back * silu).astype(bf)
        act_ref[:, 2 * span :] = (coef * (silu * up)).astype(bf)
        part = jnp.dot(act_ref[:, : 2 * span], cat_ref[...], preferred_element_type=f32).astype(bf)
        for c, ref in enumerate((near_ref, away_ref)):
            for z in range(n_near):
                for g in range(n_group):
                    at = c * half + z * block + g * 8
                    ref[g, z] = part[at : at + 8]

    sums = jax.ShapeDtypeStruct((n_group, n_near, 8, width), bf)
    return pl.pallas_call(
        kernel,
        out_shape=(
            jax.ShapeDtypeStruct((tall, 3 * span), bf),
            sums,
            sums,
            jax.ShapeDtypeStruct((2, n_dp, tall, cols), bf),
        ),
        in_specs=[SMEM] + [VMEM] * (len(pieces) + 2),
        out_specs=(VMEM,) * 4,
        compiler_params=pltpu.CompilerParams(vmem_limit_bytes=12 * MIB),
        cost_estimate=pl.CostEstimate(
            flops=2 * tall * width * 5 * span, bytes_accessed=12 * MIB, transcendentals=tall * span
        ),
        name="forward",
    )(first, *pieces, cat, down)


def column_sums(place, k, n_dp, act_1, act_2, cut_1, cut_2, hid, n_exp):
    span = act_1.shape[1] // 3
    pad = span // n_exp
    cols = cut_1.shape[-1]
    tn = (((0,), (0,)), ((), ()))

    def kernel(which_ref, a_ref, b_ref, c_ref, d_ref, *outs):
        del which_ref
        act = jnp.concatenate([a_ref[...], b_ref[...]], axis=0)
        for kind in range(3):
            side = kind // 2
            x = jnp.concatenate([c_ref[side, 0], d_ref[side, 0]], axis=0)
            part = lax.dot_general(
                act[:, kind * span : (kind + 1) * span], x, tn, preferred_element_type=jnp.float32
            ).astype(jnp.bfloat16)
            for e in range(n_exp):
                outs[e][kind] = part[e * pad : e * pad + hid, :]

    fixed = lambda n: (lambda i, w: (0,) * n)
    picked = lambda i, w: (0, lax.rem(w[0] + k, n_dp), 0, 0)
    return pl.pallas_call(
        kernel,
        out_shape=(jax.ShapeDtypeStruct((3, hid, cols), jnp.bfloat16),) * n_exp,
        grid_spec=pltpu.PrefetchScalarGridSpec(
            num_scalar_prefetch=1,
            grid=(1,),
            in_specs=[
                pl.BlockSpec(act_1.shape, fixed(2)),
                pl.BlockSpec(act_2.shape, fixed(2)),
                pl.BlockSpec((2, 1) + cut_1.shape[2:], picked),
                pl.BlockSpec((2, 1) + cut_2.shape[2:], picked),
            ],
            out_specs=(pl.BlockSpec((3, hid, cols), fixed(3)),) * n_exp,
        ),
        compiler_params=pltpu.CompilerParams(vmem_limit_bytes=8 * MIB),
        cost_estimate=pl.CostEstimate(
            flops=2 * 512 * 3 * span * cols, bytes_accessed=4 * MIB, transcendentals=0
        ),
        name="column_sums",
    )(place, act_1, act_2, cut_1, cut_2)


def finish(parts):
    n_exp = len(parts)
    _, hid, cols = parts[0][0].shape

    def kernel(*refs):
        outs = refs[-3:]
        at = 0
        for e in range(n_exp):
            mine = refs[at : at + len(parts[e])]
            at += len(parts[e])
            for kind in range(3):
                total = mine[0][kind].astype(jnp.float32)
                for r in mine[1:]:
                    total = total + r[kind].astype(jnp.float32)
                outs[kind][:, e, :] = total.astype(jnp.bfloat16)

    flat = [a for p in parts for a in p]
    outs = pl.pallas_call(
        kernel,
        grid=(pl.cdiv(cols, 2 * LANE),),
        out_shape=(jax.ShapeDtypeStruct((hid, n_exp, cols), jnp.bfloat16),) * 3,
        in_specs=[pl.BlockSpec((3, hid, 2 * LANE), lambda i: (0, 0, i)) for _ in flat],
        out_specs=(pl.BlockSpec((hid, n_exp, 2 * LANE), lambda i: (0, 0, i)),) * 3,
        compiler_params=pltpu.CompilerParams(vmem_limit_bytes=12 * MIB),
        name="finish",
    )(*flat)
    return tuple(o.transpose(1, 0, 2) for o in outs)


def small(kernel, out_shape, operands, name):
    return pl.pallas_call(
        kernel,
        out_shape=out_shape,
        in_specs=[VMEM] * len(operands),
        out_specs=jax.tree.map(lambda _: VMEM, out_shape),
        compiler_params=pltpu.CompilerParams(vmem_limit_bytes=4 * MIB),
        name=name,
    )(*operands)


def halves(lo, hi):
    lead, rows, width = lo.shape
    half = rows // 2

    def kernel(lo_ref, hi_ref, top_ref, bottom_ref):
        top_ref[...] = lo_ref[:, :half, :]
        bottom_ref[...] = hi_ref[:, half:, :]

    piece = jax.ShapeDtypeStruct((lead, half, width), lo.dtype)
    return small(kernel, (piece, piece), (lo, hi), "halves")


def add(a, b, after):
    def kernel(a_ref, b_ref, _, out_ref):
        for k in range(a.shape[0]):
            out_ref[k] = (a_ref[k].astype(jnp.float32) + b_ref[k].astype(jnp.float32)).astype(a.dtype)

    return pl.pallas_call(
        kernel,
        out_shape=jax.ShapeDtypeStruct(a.shape, a.dtype),
        in_specs=[VMEM, VMEM, pl.BlockSpec(memory_space=pl.ANY)],
        out_specs=VMEM,
        compiler_params=pltpu.CompilerParams(vmem_limit_bytes=4 * MIB),
        name="add",
    )(a, b, after)


def merge_cores(near, arrived):
    n_group = near[0].shape[0]
    chips = sum(a.shape[1] for a in near)

    def kernel(*refs):
        outs = refs[4:]
        at = 0
        for a_ref, b_ref in zip(refs[:2], refs[2:4]):
            for j in range(a_ref.shape[1]):
                for k in range(n_group):
                    total = a_ref[k, j].astype(jnp.float32) + b_ref[k, j].astype(jnp.float32)
                    outs[k][at] = total.astype(jnp.bfloat16)
                at += 1

    one = jax.ShapeDtypeStruct((chips,) + near[0].shape[2:], near[0].dtype)
    return small(kernel, (one,) * n_group, (*near, *arrived), "merge_cores")


def by_chip(parts):
    chips = parts[0].shape[0]

    def kernel(*refs):
        for j in range(chips):
            total = refs[0][j].astype(jnp.float32)
            for r in refs[1 : len(parts)]:
                total = total + r[j].astype(jnp.float32)
            refs[len(parts) + j][...] = total.astype(jnp.bfloat16)

    one = jax.ShapeDtypeStruct(parts[0].shape[1:], parts[0].dtype)
    return small(kernel, (one,) * chips, tuple(parts), "by_chip")


def total_of(parts):
    rows, width = parts[0].shape

    def kernel(*refs):
        total = refs[0][...].astype(jnp.float32)
        for r in refs[1:-1]:
            total = total + r[...].astype(jnp.float32)
        refs[-1][...] = total.astype(jnp.bfloat16)

    return small(kernel, jax.ShapeDtypeStruct((rows, width), jnp.bfloat16), tuple(parts), "total_of")


def shifted(x, axis, step):
    n = lax.axis_size(axis)
    return lax.ppermute(x, axis, [(i, (i - step) % n) for i in range(n)])


def partner(x):
    n = lax.axis_size("member")
    return lax.ppermute(x, "member", [(i, i ^ 1) for i in range(n)])


def on_device(tokens, cotangent, expert_ids, gate_weights, w_gate, w_up, w_down):
    n_group = lax.axis_size("group")
    n_dp = lax.axis_size("dp")
    n_exp, hid, width = w_gate.shape
    rows = tokens.shape[0]
    padded = up_to(width, LANE)
    place = lax.axis_index("dp").astype(jnp.int32).reshape(1)
    first = (lax.axis_index("group") * n_exp).astype(jnp.int32).reshape(1)
    mine = prepare(tokens, cotangent, expert_ids, gate_weights, n_exp * n_group, padded)
    mine, place, first = lax.optimization_barrier((mine, place, first))
    own = join([mine] + [shifted(mine, "group", k) for k in range(1, n_group)])
    lo, hi, lo_far, hi_far = [own], [own], [], []
    own_far = partner(own)
    cat, down = pack_weights(w_gate, w_up, w_down)
    for step in range(3):
        lo.append(shifted(lo[-1], "member", -2))
        hi.append(shifted(hi[-1], "member", 2))
        if step == 0:
            lo[-1], hi[-1], cat, down = lax.optimization_barrier((lo[-1], hi[-1], cat, down))
        lo_far.append(partner(lo[-1]))
        hi_far.append(partner(hi[-1]))
    top, bottom = halves(lo[3], hi[3])
    top = shifted(top, "member", -2)
    bottom = shifted(bottom, "member", 2)
    act_1, near_1, away_1, cut_1 = forward(
        [own, lo[1], hi[1], lo[2], hi[2]],
        [own_far, lo_far[0], hi_far[0], lo_far[1], hi_far[1]],
        first, cat, down, width, n_exp, n_group, n_dp,
    )
    top, bottom, act_1 = lax.optimization_barrier((top, bottom, act_1))
    act_2, near_2, away_2, cut_2 = forward(
        [lo[3], hi[3], top, bottom],
        [lo_far[2], hi_far[2], partner(top), partner(bottom)],
        first, cat, down, width, n_exp, n_group, n_dp,
    )
    def share(k):
        return column_sums(place, k, n_dp, act_1, act_2, cut_1, cut_2, hid, n_exp)

    far_0, far_1 = share(2)
    right_0 = shifted(far_0, "dp", -1)
    left_1 = shifted(far_1, "dp", 1)
    next_0, next_1 = share(1)
    prev_0, prev_1 = share(3)
    near_1, away_1, near_2, away_2, next_1, prev_0 = lax.optimization_barrier(
        (near_1, away_1, near_2, away_2, next_1, prev_0)
    )
    from_left_1 = shifted(next_1, "dp", -1)
    from_right_0 = shifted(prev_0, "dp", 1)
    here_0, here_1 = share(0)
    both = merge_cores((near_1, near_2), (partner(away_1), partner(away_2)))
    from_left_0 = shifted(add(next_0, right_0, both[0]), "dp", -1)
    from_right_1 = shifted(add(prev_1, left_1, both[0]), "dp", 1)
    grads = finish([[here_0, from_right_0, from_left_0], [here_1, from_left_1, from_right_1]])

    chips = by_chip([both[0]] + [shifted(both[k], "group", -k) for k in range(1, n_group)])
    arrived = [shifted(chips[j], "member", -2 * OFFSETS[j]) for j in range(1, len(OFFSETS))]
    grad_tokens = total_of([chips[0]] + arrived)
    return (grad_tokens,) + tuple(grads)


def solution(mesh):
    placed = P(("dp", "group", "member"), None)
    weight = P("group", "member", None)
    grad = P("group", "member", "dp")
    return jax.shard_map(
        on_device,
        mesh=mesh,
        in_specs=(placed, placed, placed, placed, weight, weight, weight),
        out_specs=(placed, grad, grad, grad),
        check_vma=False,
    )
```

```python
import jax
import jax.numpy as jnp
from jax import lax
from jax.experimental import pallas as pl
from jax.experimental.pallas import tpu as pltpu
from jax.sharding import PartitionSpec as P


LANE = 128
PAD = 64
MIB = 1 << 20
OFFSETS = (0, -1, 1, -2, 2, -3, 3, 4)
VMEM = pl.BlockSpec(memory_space=pltpu.VMEM)
SMEM = pl.BlockSpec(memory_space=pltpu.SMEM)


def up_to(n, k):
    return -(-n // k) * k


def prepare(tokens, cotangent, expert_ids, gate_weights, padded):
    rows, width = tokens.shape
    room = padded - width
    quarter = room // 4
    bf = jnp.bfloat16

    def kernel(*refs):
        out_ref, sems = refs[4], refs[9]
        copies = [pltpu.make_async_copy(refs[i], refs[5 + i], sems.at[i]) for i in range(4)]
        for copy in copies:
            copy.start()
        for copy in copies:
            copy.wait()
        tok_ref, cot_ref, id_ref, weight_ref = refs[5:9]
        lane = lax.broadcasted_iota(jnp.int32, (rows, room), 1)
        expert = jnp.where(lane < quarter, lane, lane - quarter)
        diagonal = lax.broadcasted_iota(jnp.int32, (rows, rows), 0) == lax.broadcasted_iota(jnp.int32, (rows, rows), 1)
        coef = jnp.zeros((rows, room), jnp.float32)
        for k in range(id_ref.shape[0]):
            ids = jnp.sum(jnp.where(diagonal, id_ref[k : k + 1, :], 0), axis=1, keepdims=True)
            weights = jnp.sum(jnp.where(diagonal, weight_ref[k : k + 1, :], 0.0), axis=1, keepdims=True)
            coef = coef + jnp.where(ids == expert, weights, 0.0)
        high = coef.astype(bf).astype(jnp.float32)
        tail = jnp.where(lane < quarter, high, jnp.where(lane < 2 * quarter, coef - high, 0.0))
        out_ref[0, :, :width] = tok_ref[...]
        out_ref[0, :, width:] = tail.astype(bf)
        out_ref[1, :, :width] = cot_ref[...]
        out_ref[1, :, width:] = jnp.zeros((rows, room), bf)

    operands = (tokens, cotangent, expert_ids.T, gate_weights.T)
    return pl.pallas_call(
        kernel,
        out_shape=jax.ShapeDtypeStruct((2, rows, padded), bf),
        in_specs=[pl.BlockSpec(memory_space=pltpu.HBM)] * 4,
        out_specs=VMEM,
        scratch_shapes=[pltpu.VMEM(x.shape, x.dtype) for x in operands] + [pltpu.SemaphoreType.DMA((4,))],
        name="prepare",
    )(*operands)


def join(pieces):
    lead, rows, width = pieces[0].shape

    def kernel(*refs):
        for i, ref in enumerate(refs[:-1]):
            refs[-1][:, i * rows : (i + 1) * rows, :] = ref[...]

    return pl.pallas_call(
        kernel,
        out_shape=jax.ShapeDtypeStruct((lead, rows * len(pieces), width), pieces[0].dtype),
        compiler_params=pltpu.CompilerParams(vmem_limit_bytes=4 * MIB),
        name="join",
    )(*pieces)


def pack_weights(w_gate, w_up, w_down):
    n_exp, hid, width = w_gate.shape
    pad = up_to(hid, PAD)

    def kernel(g_ref, u_ref, d_ref, cat_ref, down_ref):
        i = pl.program_id(0)
        zero = jnp.zeros((pad - hid, width), jnp.bfloat16)
        cat_ref[hid:, :] = zero
        down_ref[hid:, :] = zero
        down_ref[:hid, :] = d_ref[0]

        @pl.when(i < n_exp)
        def _():
            cat_ref[:hid, :] = g_ref[0]

        @pl.when(i >= n_exp)
        def _():
            cat_ref[:hid, :] = u_ref[0]

    return pl.pallas_call(
        kernel,
        grid=(2 * n_exp,),
        out_shape=(
            jax.ShapeDtypeStruct((2 * n_exp * pad, width), jnp.bfloat16),
            jax.ShapeDtypeStruct((n_exp * pad, width), jnp.bfloat16),
        ),
        in_specs=[
            pl.BlockSpec((1, hid, width), lambda i: (jnp.minimum(i, n_exp - 1), 0, 0)),
            pl.BlockSpec((1, hid, width), lambda i: (jnp.maximum(i - n_exp, 0), 0, 0)),
            pl.BlockSpec((1, hid, width), lambda i: (i // 2, 0, 0)),
        ],
        out_specs=(
            pl.BlockSpec((pad, width), lambda i: (i, 0)),
            pl.BlockSpec((pad, width), lambda i: (i // 2, 0)),
        ),
        compiler_params=pltpu.CompilerParams(vmem_limit_bytes=14 * MIB),
        name="pack_weights",
    )(w_gate, w_up, w_down)


def forward(own, far, first, cat, down, width, n_exp, n_group, n_dp):
    half = sum(p.shape[1] for p in own)
    tall = 2 * half
    span = down.shape[0]
    pad = span // n_exp
    cols = width // n_dp
    bf = jnp.bfloat16
    f32 = jnp.float32
    nt = (((1,), (1,)), ((), ()))
    pieces = tuple(own) + tuple(far)
    block = 8 * n_group
    n_near = half // block

    def kernel(first_ref, *refs):
        rows = refs[: len(pieces)]
        cat_ref, down_ref, act_ref, near_ref, away_ref, cut_ref = refs[len(pieces) :]
        x = jnp.concatenate([r[0, :, :width] for r in rows], axis=0)
        y = jnp.concatenate([r[1, :, :width] for r in rows], axis=0)
        pre = lax.dot_general(x, cat_ref[...], nt, preferred_element_type=f32)
        back = lax.dot_general(y, down_ref[...], nt, preferred_element_type=f32)
        for d in range(n_dp):
            cut_ref[0, d] = x[:, d * cols : (d + 1) * cols]
            cut_ref[1, d] = y[:, d * cols : (d + 1) * cols]
        gate = pre[:, :span]
        up = pre[:, span:]
        tail = jnp.concatenate([r[0, :, width:] for r in rows], axis=0).astype(f32)
        lanes = lax.broadcasted_iota(jnp.int32, tail.shape, 1)
        quarter = tail.shape[1] // 4
        column = lax.broadcasted_iota(jnp.int32, gate.shape, 1)
        coef = jnp.zeros_like(gate)
        for e in range(n_exp):
            wanted = first_ref[0] + e
            hit = (lanes == wanted) | (lanes == wanted + quarter)
            mine = jnp.sum(jnp.where(hit, tail, 0.0), axis=1, keepdims=True)
            coef = jnp.where((column >= e * pad) & (column < (e + 1) * pad), mine, coef)
        sig = jax.nn.sigmoid(gate)
        silu = gate * sig
        back = back * coef
        act_ref[:, :span] = (back * up * sig * (1.0 + gate * (1.0 - sig))).astype(bf)
        act_ref[:, span : 2 * span] = (back * silu).astype(bf)
        act_ref[:, 2 * span :] = (coef * (silu * up)).astype(bf)
        part = jnp.dot(act_ref[:, : 2 * span], cat_ref[...], preferred_element_type=f32).astype(bf)
        for c, ref in enumerate((near_ref, away_ref)):
            for z in range(n_near):
                for g in range(n_group):
                    at = c * half + z * block + g * 8
                    ref[g, z] = part[at : at + 8]

    sums = jax.ShapeDtypeStruct((n_group, n_near, 8, width), bf)
    return pl.pallas_call(
        kernel,
        out_shape=(
            jax.ShapeDtypeStruct((tall, 3 * span), bf),
            sums,
            sums,
            jax.ShapeDtypeStruct((2, n_dp, tall, cols), bf),
        ),
        in_specs=[SMEM] + [VMEM] * (len(pieces) + 2),
        out_specs=(VMEM,) * 4,
        compiler_params=pltpu.CompilerParams(vmem_limit_bytes=12 * MIB),
        cost_estimate=pl.CostEstimate(
            flops=2 * tall * width * 5 * span, bytes_accessed=12 * MIB, transcendentals=tall * span
        ),
        name="forward",
    )(first, *pieces, cat, down)


def column_sums(place, offsets, n_dp, act_1, act_2, cut_1, cut_2, hid, n_exp, after=()):
    span = act_1.shape[1] // 3
    pad = span // n_exp
    cols = cut_1.shape[-1]
    tn = (((0,), (0,)), ((), ()))
    count = len(offsets)

    def kernel(place_ref, a_ref, b_ref, c_ref, d_ref, *rest):
        del place_ref
        outs = rest[len(after) :]
        act = jnp.concatenate([a_ref[...], b_ref[...]], axis=0)
        for kind in range(3):
            side = kind // 2
            x = jnp.concatenate([c_ref[side, 0], d_ref[side, 0]], axis=0)
            part = lax.dot_general(
                act[:, kind * span : (kind + 1) * span], x, tn, preferred_element_type=jnp.float32
            ).astype(jnp.bfloat16)
            for step in range(count):

                @pl.when(pl.program_id(0) == step)
                def _(step=step):
                    for e in range(n_exp):
                        outs[step * n_exp + e][kind] = part[e * pad : e * pad + hid, :]

    def picked(i, w):
        k = offsets[0]
        for step in range(1, count):
            k = jnp.where(i == step, offsets[step], k)
        return (0, lax.rem(w[0] + k, n_dp), 0, 0)

    fixed = lambda n: (lambda i, w: (0,) * n)
    outs = pl.pallas_call(
        kernel,
        out_shape=(jax.ShapeDtypeStruct((3, hid, cols), jnp.bfloat16),) * (n_exp * count),
        grid_spec=pltpu.PrefetchScalarGridSpec(
            num_scalar_prefetch=1,
            grid=(count,),
            in_specs=[
                pl.BlockSpec(act_1.shape, fixed(2)),
                pl.BlockSpec(act_2.shape, fixed(2)),
                pl.BlockSpec((2, 1) + cut_1.shape[2:], picked),
                pl.BlockSpec((2, 1) + cut_2.shape[2:], picked),
            ]
            + [pl.BlockSpec(memory_space=pl.ANY)] * len(after),
            out_specs=(VMEM,) * (n_exp * count),
        ),
        compiler_params=pltpu.CompilerParams(vmem_limit_bytes=12 * MIB),
        cost_estimate=pl.CostEstimate(
            flops=2 * 512 * 3 * span * cols * count, bytes_accessed=4 * MIB * count, transcendentals=0
        ),
        name="column_sums",
    )(place, act_1, act_2, cut_1, cut_2, *after)
    return [outs[i * n_exp : (i + 1) * n_exp] for i in range(count)]


def finish(parts):
    n_exp = len(parts)
    _, hid, cols = parts[0][0].shape

    def kernel(*refs):
        outs = refs[-3:]
        at = 0
        for e in range(n_exp):
            mine = refs[at : at + len(parts[e])]
            at += len(parts[e])
            for kind in range(3):
                total = mine[0][kind].astype(jnp.float32)
                for r in mine[1:]:
                    total = total + r[kind].astype(jnp.float32)
                outs[kind][:, e, :] = total.astype(jnp.bfloat16)

    flat = [a for p in parts for a in p]
    outs = pl.pallas_call(
        kernel,
        grid=(pl.cdiv(cols, 2 * LANE),),
        out_shape=(jax.ShapeDtypeStruct((hid, n_exp, cols), jnp.bfloat16),) * 3,
        in_specs=[pl.BlockSpec((3, hid, 2 * LANE), lambda i: (0, 0, i)) for _ in flat],
        out_specs=(pl.BlockSpec((hid, n_exp, 2 * LANE), lambda i: (0, 0, i)),) * 3,
        compiler_params=pltpu.CompilerParams(vmem_limit_bytes=12 * MIB),
        name="finish",
    )(*flat)
    return tuple(o.transpose(1, 0, 2) for o in outs)


def small(kernel, out_shape, operands):
    return pl.pallas_call(
        kernel,
        out_shape=out_shape,
        in_specs=[VMEM] * len(operands),
        out_specs=jax.tree.map(lambda _: VMEM, out_shape),
        compiler_params=pltpu.CompilerParams(vmem_limit_bytes=4 * MIB),
    )(*operands)


def halves(lo, hi):
    lead, rows, width = lo.shape
    half = rows // 2

    def kernel(lo_ref, hi_ref, top_ref, bottom_ref):
        top_ref[...] = lo_ref[:, :half, :]
        bottom_ref[...] = hi_ref[:, half:, :]

    piece = jax.ShapeDtypeStruct((lead, half, width), lo.dtype)
    return small(kernel, (piece, piece), (lo, hi))


def add(a, b, after):
    def kernel(a_ref, b_ref, _, out_ref):
        for k in range(a.shape[0]):
            out_ref[k] = (a_ref[k].astype(jnp.float32) + b_ref[k].astype(jnp.float32)).astype(a.dtype)

    return pl.pallas_call(
        kernel,
        out_shape=jax.ShapeDtypeStruct(a.shape, a.dtype),
        in_specs=[VMEM, VMEM, pl.BlockSpec(memory_space=pl.ANY)],
        out_specs=VMEM,
        compiler_params=pltpu.CompilerParams(vmem_limit_bytes=4 * MIB),
        name="add",
    )(a, b, after)


def merge_cores(near, arrived):
    n_group = near[0].shape[0]
    chips = sum(a.shape[1] for a in near)

    def kernel(*refs):
        outs = refs[4:]
        at = 0
        for a_ref, b_ref in zip(refs[:2], refs[2:4]):
            for j in range(a_ref.shape[1]):
                for k in range(n_group):
                    total = a_ref[k, j].astype(jnp.float32) + b_ref[k, j].astype(jnp.float32)
                    outs[k][at] = total.astype(jnp.bfloat16)
                at += 1

    one = jax.ShapeDtypeStruct((chips,) + near[0].shape[2:], near[0].dtype)
    return small(kernel, (one,) * n_group, (*near, *arrived))


def by_chip(parts):
    chips = parts[0].shape[0]
    half = chips // 2

    def kernel(*refs):
        outs = refs[len(parts) :]
        for j, offset in enumerate(OFFSETS):
            total = refs[0][j].astype(jnp.float32)
            for r in refs[1 : len(parts)]:
                total = total + r[j].astype(jnp.float32)
            ahead = offset % chips
            outs[ahead // half][ahead % half] = total.astype(jnp.bfloat16)

    one = jax.ShapeDtypeStruct((half,) + parts[0].shape[1:], parts[0].dtype)
    return small(kernel, (one, one), tuple(parts))


def fold(kept, arrived):
    half = kept.shape[0] // 2

    def kernel(a_ref, b_ref, *outs):
        for j in range(2 * half):
            total = a_ref[j].astype(jnp.float32) + b_ref[j].astype(jnp.float32)
            outs[j // half][j % half] = total.astype(jnp.bfloat16)

    one = jax.ShapeDtypeStruct((half,) + kept.shape[1:], kept.dtype)
    return small(kernel, (one, one), (kept, arrived))


def total_of(a, b):
    def kernel(a_ref, b_ref, out_ref):
        out_ref[...] = (a_ref[0].astype(jnp.float32) + b_ref[0].astype(jnp.float32)).astype(jnp.bfloat16)

    return small(kernel, jax.ShapeDtypeStruct(a.shape[1:], a.dtype), (a, b))


def shifted(x, axis, step):
    n = lax.axis_size(axis)
    return lax.ppermute(x, axis, [(i, (i - step) % n) for i in range(n)])


def partner(x):
    n = lax.axis_size("member")
    return lax.ppermute(x, "member", [(i, i ^ 1) for i in range(n)])


def step_of(tokens, cotangent, expert_ids, gate_weights, w_gate, w_up, w_down):
    n_group = lax.axis_size("group")
    n_dp = lax.axis_size("dp")
    n_exp, hid, width = w_gate.shape
    padded = up_to(width, LANE)
    place = lax.axis_index("dp").astype(jnp.int32).reshape(1)
    first = (lax.axis_index("group") * n_exp).astype(jnp.int32).reshape(1)
    mine = prepare(tokens, cotangent, expert_ids, gate_weights, padded)
    mine, place, first = lax.optimization_barrier((mine, place, first))
    own = join([mine] + [shifted(mine, "group", k) for k in range(1, n_group)])
    lo, hi, lo_far, hi_far = [own], [own], [], []
    own_far = partner(own)
    cat, down = pack_weights(w_gate, w_up, w_down)
    for step in range(3):
        lo.append(shifted(lo[-1], "member", -2))
        hi.append(shifted(hi[-1], "member", 2))
        if step == 0:
            lo[-1], hi[-1], cat, down = lax.optimization_barrier((lo[-1], hi[-1], cat, down))
        if step == 1:
            lo[-1], hi[-1], own_far, lo_far[0], hi_far[0] = lax.optimization_barrier(
                (lo[-1], hi[-1], own_far, lo_far[0], hi_far[0])
            )
        lo_far.append(partner(lo[-1]))
        hi_far.append(partner(hi[-1]))
    act_1, near_1, away_1, cut_1 = forward(
        [own, lo[1], hi[1], lo[2], hi[2]],
        [own_far, lo_far[0], hi_far[0], lo_far[1], hi_far[1]],
        first, cat, down, width, n_exp, n_group, n_dp,
    )
    lo[3], hi[3], act_1 = lax.optimization_barrier((lo[3], hi[3], act_1))
    top, bottom = halves(lo[3], hi[3])
    top = shifted(top, "member", -2)
    bottom = shifted(bottom, "member", 2)
    act_2, near_2, away_2, cut_2 = forward(
        [lo[3], hi[3], top, bottom],
        [lo_far[2], hi_far[2], partner(top), partner(bottom)],
        first, cat, down, width, n_exp, n_group, n_dp,
    )

    def shares(offsets, after=()):
        return column_sums(place, offsets, n_dp, act_1, act_2, cut_1, cut_2, hid, n_exp, after)

    ((far_0, far_1),) = shares((2,))
    right_0 = shifted(far_0, "dp", -1)
    left_1 = shifted(far_1, "dp", 1)
    (next_0, next_1), (prev_0, prev_1), (here_0, here_1) = shares((1, 3, 0), (far_0,))
    near_1, away_1, near_2, away_2, next_1, prev_0 = lax.optimization_barrier(
        (near_1, away_1, near_2, away_2, next_1, prev_0)
    )
    from_left_1 = shifted(next_1, "dp", -1)
    from_right_0 = shifted(prev_0, "dp", 1)
    both = merge_cores((near_1, near_2), (partner(away_1), partner(away_2)))
    kept, sent = by_chip([both[0]] + [shifted(both[k], "group", -k) for k in range(1, n_group)])
    from_left_0 = shifted(add(next_0, right_0, kept), "dp", -1)
    from_right_1 = shifted(add(prev_1, left_1, kept), "dp", 1)
    kept, sent = fold(kept, shifted(sent, "member", -8))
    kept, sent = fold(kept, shifted(sent, "member", -4))
    grad_tokens = total_of(kept, shifted(sent, "member", -2))
    grads = finish([[here_0, from_right_0, from_left_0], [here_1, from_left_1, from_right_1]])
    return (grad_tokens,) + tuple(grads)


def solution(mesh):
    placed = P(("dp", "group", "member"), None)
    weight = P("group", "member", None)
    grad = P("group", "member", "dp")
    return jax.shard_map(
        step_of,
        mesh=mesh,
        in_specs=(placed, placed, placed, placed, weight, weight, weight),
        out_specs=(placed, grad, grad, grad),
        check_vma=False,
    )
```

```python
import jax
import jax.numpy as jnp
from jax import lax
from jax.experimental import pallas as pl
from jax.experimental.pallas import tpu as pltpu
from jax.sharding import PartitionSpec as P


LANE = 128
PAD = 64
MIB = 1 << 20
OFFSETS = (0, -1, 1, -2, 2, -3, 3, 4)
VMEM = pl.BlockSpec(memory_space=pltpu.VMEM)
SMEM = pl.BlockSpec(memory_space=pltpu.SMEM)


def up_to(n, k):
    return -(-n // k) * k


def prepare(tokens, cotangent, expert_ids, gate_weights, padded):
    rows, width = tokens.shape
    room = padded - width
    quarter = room // 4
    bf = jnp.bfloat16

    def kernel(*refs):
        out_ref, sems = refs[4], refs[9]
        copies = [pltpu.make_async_copy(refs[i], refs[5 + i], sems.at[i]) for i in range(4)]
        for copy in copies:
            copy.start()
        for copy in copies:
            copy.wait()
        tok_ref, cot_ref, id_ref, weight_ref = refs[5:9]
        lane = lax.broadcasted_iota(jnp.int32, (rows, room), 1)
        expert = jnp.where(lane < quarter, lane, lane - quarter)
        diagonal = lax.broadcasted_iota(jnp.int32, (rows, rows), 0) == lax.broadcasted_iota(jnp.int32, (rows, rows), 1)
        coef = jnp.zeros((rows, room), jnp.float32)
        for k in range(id_ref.shape[0]):
            ids = jnp.sum(jnp.where(diagonal, id_ref[k : k + 1, :], 0), axis=1, keepdims=True)
            weights = jnp.sum(jnp.where(diagonal, weight_ref[k : k + 1, :], 0.0), axis=1, keepdims=True)
            coef = coef + jnp.where(ids == expert, weights, 0.0)
        high = coef.astype(bf).astype(jnp.float32)
        tail = jnp.where(lane < quarter, high, jnp.where(lane < 2 * quarter, coef - high, 0.0))
        out_ref[0, :, :width] = tok_ref[...]
        out_ref[0, :, width:] = tail.astype(bf)
        out_ref[1, :, :width] = cot_ref[...]
        out_ref[1, :, width:] = jnp.zeros((rows, room), bf)

    operands = (tokens, cotangent, expert_ids.T, gate_weights.T)
    return pl.pallas_call(
        kernel,
        out_shape=jax.ShapeDtypeStruct((2, rows, padded), bf),
        in_specs=[pl.BlockSpec(memory_space=pltpu.HBM)] * 4,
        out_specs=VMEM,
        scratch_shapes=[pltpu.VMEM(x.shape, x.dtype) for x in operands] + [pltpu.SemaphoreType.DMA((4,))],
        name="prepare",
    )(*operands)


def join(pieces):
    lead, rows, width = pieces[0].shape

    def kernel(*refs):
        for i, ref in enumerate(refs[:-1]):
            refs[-1][:, i * rows : (i + 1) * rows, :] = ref[...]

    return pl.pallas_call(
        kernel,
        out_shape=jax.ShapeDtypeStruct((lead, rows * len(pieces), width), pieces[0].dtype),
        compiler_params=pltpu.CompilerParams(vmem_limit_bytes=4 * MIB),
        name="join",
    )(*pieces)


def pack_weights(w_gate, w_up, w_down):
    n_exp, hid, width = w_gate.shape
    pad = up_to(hid, PAD)

    def kernel(g_ref, u_ref, d_ref, cat_ref, down_ref):
        i = pl.program_id(0)
        zero = jnp.zeros((pad - hid, width), jnp.bfloat16)
        cat_ref[hid:, :] = zero
        down_ref[hid:, :] = zero
        down_ref[:hid, :] = d_ref[0]

        @pl.when(i < n_exp)
        def _():
            cat_ref[:hid, :] = g_ref[0]

        @pl.when(i >= n_exp)
        def _():
            cat_ref[:hid, :] = u_ref[0]

    return pl.pallas_call(
        kernel,
        grid=(2 * n_exp,),
        out_shape=(
            jax.ShapeDtypeStruct((2 * n_exp * pad, width), jnp.bfloat16),
            jax.ShapeDtypeStruct((n_exp * pad, width), jnp.bfloat16),
        ),
        in_specs=[
            pl.BlockSpec((1, hid, width), lambda i: (jnp.minimum(i, n_exp - 1), 0, 0)),
            pl.BlockSpec((1, hid, width), lambda i: (jnp.maximum(i - n_exp, 0), 0, 0)),
            pl.BlockSpec((1, hid, width), lambda i: (i // 2, 0, 0)),
        ],
        out_specs=(
            pl.BlockSpec((pad, width), lambda i: (i, 0)),
            pl.BlockSpec((pad, width), lambda i: (i // 2, 0)),
        ),
        compiler_params=pltpu.CompilerParams(vmem_limit_bytes=14 * MIB),
        name="pack_weights",
    )(w_gate, w_up, w_down)


def forward(own, far, first, cat, down, width, n_exp, n_group, n_dp):
    half = sum(p.shape[1] for p in own)
    tall = 2 * half
    span = down.shape[0]
    pad = span // n_exp
    cols = width // n_dp
    bf = jnp.bfloat16
    f32 = jnp.float32
    nt = (((1,), (1,)), ((), ()))
    pieces = tuple(own) + tuple(far)
    block = 8 * n_group
    n_near = half // block

    def kernel(first_ref, *refs):
        rows = refs[: len(pieces)]
        cat_ref, down_ref, act_ref, near_ref, away_ref, cut_ref = refs[len(pieces) :]
        x = jnp.concatenate([r[0, :, :width] for r in rows], axis=0)
        y = jnp.concatenate([r[1, :, :width] for r in rows], axis=0)
        pre = lax.dot_general(x, cat_ref[...], nt, preferred_element_type=f32)
        back = lax.dot_general(y, down_ref[...], nt, preferred_element_type=f32)
        for d in range(n_dp):
            cut_ref[0, d] = x[:, d * cols : (d + 1) * cols]
            cut_ref[1, d] = y[:, d * cols : (d + 1) * cols]
        gate = pre[:, :span]
        up = pre[:, span:]
        tail = jnp.concatenate([r[0, :, width:] for r in rows], axis=0).astype(f32)
        lanes = lax.broadcasted_iota(jnp.int32, tail.shape, 1)
        quarter = tail.shape[1] // 4
        column = lax.broadcasted_iota(jnp.int32, gate.shape, 1)
        coef = jnp.zeros_like(gate)
        for e in range(n_exp):
            wanted = first_ref[0] + e
            hit = (lanes == wanted) | (lanes == wanted + quarter)
            mine = jnp.sum(jnp.where(hit, tail, 0.0), axis=1, keepdims=True)
            coef = jnp.where((column >= e * pad) & (column < (e + 1) * pad), mine, coef)
        sig = jax.nn.sigmoid(gate)
        silu = gate * sig
        back = back * coef
        act_ref[:, :span] = (back * up * sig * (1.0 + gate * (1.0 - sig))).astype(bf)
        act_ref[:, span : 2 * span] = (back * silu).astype(bf)
        act_ref[:, 2 * span :] = (coef * (silu * up)).astype(bf)
        part = jnp.dot(act_ref[:, : 2 * span], cat_ref[...], preferred_element_type=f32).astype(bf)
        for c, ref in enumerate((near_ref, away_ref)):
            for z in range(n_near):
                for g in range(n_group):
                    at = c * half + z * block + g * 8
                    ref[g, z] = part[at : at + 8]

    sums = jax.ShapeDtypeStruct((n_group, n_near, 8, width), bf)
    return pl.pallas_call(
        kernel,
        out_shape=(
            jax.ShapeDtypeStruct((tall, 3 * span), bf),
            sums,
            sums,
            jax.ShapeDtypeStruct((2, n_dp, tall, cols), bf),
        ),
        in_specs=[SMEM] + [VMEM] * (len(pieces) + 2),
        out_specs=(VMEM,) * 4,
        compiler_params=pltpu.CompilerParams(vmem_limit_bytes=12 * MIB),
        cost_estimate=pl.CostEstimate(
            flops=2 * tall * width * 5 * span, bytes_accessed=12 * MIB, transcendentals=tall * span
        ),
        name="forward",
    )(first, *pieces, cat, down)


def column_sums(place, offsets, n_dp, act_1, act_2, cut_1, cut_2, hid, n_exp, after=()):
    span = act_1.shape[1] // 3
    pad = span // n_exp
    cols = cut_1.shape[-1]
    tn = (((0,), (0,)), ((), ()))
    count = len(offsets)

    def kernel(place_ref, a_ref, b_ref, c_ref, d_ref, *rest):
        del place_ref
        outs = rest[len(after) :]
        act = jnp.concatenate([a_ref[...], b_ref[...]], axis=0)
        for kind in range(3):
            side = kind // 2
            x = jnp.concatenate([c_ref[side, 0], d_ref[side, 0]], axis=0)
            part = lax.dot_general(
                act[:, kind * span : (kind + 1) * span], x, tn, preferred_element_type=jnp.float32
            ).astype(jnp.bfloat16)
            for step in range(count):

                @pl.when(pl.program_id(0) == step)
                def _(step=step):
                    for e in range(n_exp):
                        outs[step * n_exp + e][kind] = part[e * pad : e * pad + hid, :]

    def picked(i, w):
        k = offsets[0]
        for step in range(1, count):
            k = jnp.where(i == step, offsets[step], k)
        return (0, lax.rem(w[0] + k, n_dp), 0, 0)

    fixed = lambda n: (lambda i, w: (0,) * n)
    outs = pl.pallas_call(
        kernel,
        out_shape=(jax.ShapeDtypeStruct((3, hid, cols), jnp.bfloat16),) * (n_exp * count),
        grid_spec=pltpu.PrefetchScalarGridSpec(
            num_scalar_prefetch=1,
            grid=(count,),
            in_specs=[
                pl.BlockSpec(act_1.shape, fixed(2)),
                pl.BlockSpec(act_2.shape, fixed(2)),
                pl.BlockSpec((2, 1) + cut_1.shape[2:], picked),
                pl.BlockSpec((2, 1) + cut_2.shape[2:], picked),
            ]
            + [pl.BlockSpec(memory_space=pl.ANY)] * len(after),
            out_specs=(VMEM,) * (n_exp * count),
        ),
        compiler_params=pltpu.CompilerParams(vmem_limit_bytes=12 * MIB),
        cost_estimate=pl.CostEstimate(
            flops=2 * 512 * 3 * span * cols * count, bytes_accessed=4 * MIB * count, transcendentals=0
        ),
        name="column_sums",
    )(place, act_1, act_2, cut_1, cut_2, *after)
    return [outs[i * n_exp : (i + 1) * n_exp] for i in range(count)]


def finish(parts):
    n_exp = len(parts)
    _, hid, cols = parts[0][0].shape

    def kernel(*refs):
        outs = refs[-3:]
        at = 0
        for e in range(n_exp):
            mine = refs[at : at + len(parts[e])]
            at += len(parts[e])
            for kind in range(3):
                total = mine[0][kind].astype(jnp.float32)
                for r in mine[1:]:
                    total = total + r[kind].astype(jnp.float32)
                outs[kind][:, e, :] = total.astype(jnp.bfloat16)

    flat = [a for p in parts for a in p]
    outs = pl.pallas_call(
        kernel,
        grid=(pl.cdiv(cols, 2 * LANE),),
        out_shape=(jax.ShapeDtypeStruct((hid, n_exp, cols), jnp.bfloat16),) * 3,
        in_specs=[pl.BlockSpec((3, hid, 2 * LANE), lambda i: (0, 0, i)) for _ in flat],
        out_specs=(pl.BlockSpec((hid, n_exp, 2 * LANE), lambda i: (0, 0, i)),) * 3,
        compiler_params=pltpu.CompilerParams(vmem_limit_bytes=12 * MIB),
        name="finish",
    )(*flat)
    return tuple(o.transpose(1, 0, 2) for o in outs)


def small(kernel, out_shape, operands):
    return pl.pallas_call(
        kernel,
        out_shape=out_shape,
        in_specs=[VMEM] * len(operands),
        out_specs=jax.tree.map(lambda _: VMEM, out_shape),
        compiler_params=pltpu.CompilerParams(vmem_limit_bytes=4 * MIB),
    )(*operands)


def halves(lo, hi):
    lead, rows, width = lo.shape
    half = rows // 2

    def kernel(lo_ref, hi_ref, top_ref, bottom_ref):
        top_ref[...] = lo_ref[:, :half, :]
        bottom_ref[...] = hi_ref[:, half:, :]

    piece = jax.ShapeDtypeStruct((lead, half, width), lo.dtype)
    return small(kernel, (piece, piece), (lo, hi))


def add(a, b, after):
    def kernel(a_ref, b_ref, _, out_ref):
        for k in range(a.shape[0]):
            out_ref[k] = (a_ref[k].astype(jnp.float32) + b_ref[k].astype(jnp.float32)).astype(a.dtype)

    return pl.pallas_call(
        kernel,
        out_shape=jax.ShapeDtypeStruct(a.shape, a.dtype),
        in_specs=[VMEM, VMEM, pl.BlockSpec(memory_space=pl.ANY)],
        out_specs=VMEM,
        compiler_params=pltpu.CompilerParams(vmem_limit_bytes=4 * MIB),
        name="add",
    )(a, b, after)


def merge_cores(near, arrived):
    n_group = near[0].shape[0]
    chips = sum(a.shape[1] for a in near)

    def kernel(*refs):
        outs = refs[4:]
        at = 0
        for a_ref, b_ref in zip(refs[:2], refs[2:4]):
            for j in range(a_ref.shape[1]):
                for k in range(n_group):
                    total = a_ref[k, j].astype(jnp.float32) + b_ref[k, j].astype(jnp.float32)
                    outs[k][at] = total.astype(jnp.bfloat16)
                at += 1

    one = jax.ShapeDtypeStruct((chips,) + near[0].shape[2:], near[0].dtype)
    return small(kernel, (one,) * n_group, (*near, *arrived))


def by_chip(parts):
    chips = parts[0].shape[0]
    half = chips // 2

    def kernel(*refs):
        outs = refs[len(parts) :]
        for j, offset in enumerate(OFFSETS):
            total = refs[0][j].astype(jnp.float32)
            for r in refs[1 : len(parts)]:
                total = total + r[j].astype(jnp.float32)
            ahead = offset % chips
            outs[ahead // half][ahead % half] = total.astype(jnp.bfloat16)

    one = jax.ShapeDtypeStruct((half,) + parts[0].shape[1:], parts[0].dtype)
    return small(kernel, (one, one), tuple(parts))


def fold(kept, arrived):
    half = kept.shape[0] // 2

    def kernel(a_ref, b_ref, *outs):
        for j in range(2 * half):
            total = a_ref[j].astype(jnp.float32) + b_ref[j].astype(jnp.float32)
            outs[j // half][j % half] = total.astype(jnp.bfloat16)

    one = jax.ShapeDtypeStruct((half,) + kept.shape[1:], kept.dtype)
    return small(kernel, (one, one), (kept, arrived))


def total_of(a, b):
    def kernel(a_ref, b_ref, out_ref):
        out_ref[...] = (a_ref[0].astype(jnp.float32) + b_ref[0].astype(jnp.float32)).astype(jnp.bfloat16)

    return small(kernel, jax.ShapeDtypeStruct(a.shape[1:], a.dtype), (a, b))


def shifted(x, axis, step):
    n = lax.axis_size(axis)
    return lax.ppermute(x, axis, [(i, (i - step) % n) for i in range(n)])


def partner(x):
    n = lax.axis_size("member")
    return lax.ppermute(x, "member", [(i, i ^ 1) for i in range(n)])


def step_of(tokens, cotangent, expert_ids, gate_weights, w_gate, w_up, w_down):
    n_group = lax.axis_size("group")
    n_dp = lax.axis_size("dp")
    n_exp, hid, width = w_gate.shape
    padded = up_to(width, LANE)
    place = lax.axis_index("dp").astype(jnp.int32).reshape(1)
    first = (lax.axis_index("group") * n_exp).astype(jnp.int32).reshape(1)
    mine = prepare(tokens, cotangent, expert_ids, gate_weights, padded)
    mine, place, first = lax.optimization_barrier((mine, place, first))
    own = join([mine] + [shifted(mine, "group", k) for k in range(1, n_group)])
    lo, hi, lo_far, hi_far = [own], [own], [], []
    own_far = partner(own)
    cat, down = pack_weights(w_gate, w_up, w_down)
    for step in range(3):
        lo.append(shifted(lo[-1], "member", -2))
        hi.append(shifted(hi[-1], "member", 2))
        if step == 0:
            lo[-1], hi[-1], cat, down = lax.optimization_barrier((lo[-1], hi[-1], cat, down))
        if step == 1:
            lo[-1], hi[-1], own_far, lo_far[0], hi_far[0] = lax.optimization_barrier(
                (lo[-1], hi[-1], own_far, lo_far[0], hi_far[0])
            )
        lo_far.append(partner(lo[-1]))
        hi_far.append(partner(hi[-1]))
    act_1, near_1, away_1, cut_1 = forward(
        [own, lo[1], hi[1], lo[2], hi[2]],
        [own_far, lo_far[0], hi_far[0], lo_far[1], hi_far[1]],
        first, cat, down, width, n_exp, n_group, n_dp,
    )
    top, bottom = halves(lo[3], hi[3])
    top = shifted(top, "member", -2)
    bottom = shifted(bottom, "member", 2)
    act_2, near_2, away_2, cut_2 = forward(
        [lo[3], hi[3], top, bottom],
        [lo_far[2], hi_far[2], partner(top), partner(bottom)],
        first, cat, down, width, n_exp, n_group, n_dp,
    )

    def shares(offsets, after=()):
        return column_sums(place, offsets, n_dp, act_1, act_2, cut_1, cut_2, hid, n_exp, after)

    ((far_0, far_1),) = shares((2,))
    right_0 = shifted(far_0, "dp", -1)
    left_1 = shifted(far_1, "dp", 1)
    away_1 = partner(away_1)
    away_2 = partner(away_2)
    both = merge_cores((near_1, near_2), (away_1, away_2))
    others = []
    for k in range(1, n_group):
        others.append(shifted(both[k], "group", -k))
    (next_0, next_1), (prev_0, prev_1), (here_0, here_1) = shares((1, 3, 0), (far_0,))
    from_left_1 = shifted(next_1, "dp", -1)
    from_right_0 = shifted(prev_0, "dp", 1)
    kept, sent = by_chip([both[0]] + others)
    from_left_0 = shifted(add(next_0, right_0, kept), "dp", -1)
    from_right_1 = shifted(add(prev_1, left_1, kept), "dp", 1)
    kept, sent = fold(kept, shifted(sent, "member", -8))
    kept, sent = fold(kept, shifted(sent, "member", -4))
    grad_tokens = total_of(kept, shifted(sent, "member", -2))
    grads = finish([[here_0, from_right_0, from_left_0], [here_1, from_left_1, from_right_1]])
    return (grad_tokens,) + tuple(grads)


def solution(mesh):
    placed = P(("dp", "group", "member"), None)
    weight = P("group", "member", None)
    grad = P("group", "member", "dp")
    return jax.shard_map(
        step_of,
        mesh=mesh,
        in_specs=(placed, placed, placed, placed, weight, weight, weight),
        out_specs=(placed, grad, grad, grad),
        check_vma=False,
    )
```

```python
import jax
import jax.numpy as jnp
from jax import lax
from jax.experimental import pallas as pl
from jax.experimental.pallas import tpu as pltpu
from jax.sharding import PartitionSpec as P


LANE = 128
PAD = 64
MIB = 1 << 20
OFFSETS = (0, -1, 1, -2, 2, -3, 3, 4)
VMEM = pl.BlockSpec(memory_space=pltpu.VMEM)
SMEM = pl.BlockSpec(memory_space=pltpu.SMEM)


def up_to(n, k):
    return -(-n // k) * k


def prepare(tokens, cotangent, expert_ids, gate_weights, padded):
    rows, width = tokens.shape
    room = padded - width
    quarter = room // 4
    bf = jnp.bfloat16

    def kernel(*refs):
        out_ref, sems = refs[4], refs[9]
        copies = [pltpu.make_async_copy(refs[i], refs[5 + i], sems.at[i]) for i in range(4)]
        for copy in copies:
            copy.start()
        for copy in copies:
            copy.wait()
        tok_ref, cot_ref, id_ref, weight_ref = refs[5:9]
        lane = lax.broadcasted_iota(jnp.int32, (rows, room), 1)
        expert = jnp.where(lane < quarter, lane, lane - quarter)
        diagonal = lax.broadcasted_iota(jnp.int32, (rows, rows), 0) == lax.broadcasted_iota(jnp.int32, (rows, rows), 1)
        coef = jnp.zeros((rows, room), jnp.float32)
        for k in range(id_ref.shape[0]):
            ids = jnp.sum(jnp.where(diagonal, id_ref[k : k + 1, :], 0), axis=1, keepdims=True)
            weights = jnp.sum(jnp.where(diagonal, weight_ref[k : k + 1, :], 0.0), axis=1, keepdims=True)
            coef = coef + jnp.where(ids == expert, weights, 0.0)
        high = coef.astype(bf).astype(jnp.float32)
        tail = jnp.where(lane < quarter, high, jnp.where(lane < 2 * quarter, coef - high, 0.0))
        out_ref[0, :, :width] = tok_ref[...]
        out_ref[0, :, width:] = tail.astype(bf)
        out_ref[1, :, :width] = cot_ref[...]
        out_ref[1, :, width:] = jnp.zeros((rows, room), bf)

    operands = (tokens, cotangent, expert_ids.T, gate_weights.T)
    return pl.pallas_call(
        kernel,
        out_shape=jax.ShapeDtypeStruct((2, rows, padded), bf),
        in_specs=[pl.BlockSpec(memory_space=pltpu.HBM)] * 4,
        out_specs=VMEM,
        scratch_shapes=[pltpu.VMEM(x.shape, x.dtype) for x in operands] + [pltpu.SemaphoreType.DMA((4,))],
        name="prepare",
    )(*operands)


def join(pieces):
    lead, rows, width = pieces[0].shape

    def kernel(*refs):
        for i, ref in enumerate(refs[:-1]):
            refs[-1][:, i * rows : (i + 1) * rows, :] = ref[...]

    return pl.pallas_call(
        kernel,
        out_shape=jax.ShapeDtypeStruct((lead, rows * len(pieces), width), pieces[0].dtype),
        compiler_params=pltpu.CompilerParams(vmem_limit_bytes=4 * MIB),
        name="join",
    )(*pieces)


def pack_weights(w_gate, w_up, w_down):
    n_exp, hid, width = w_gate.shape
    pad = up_to(hid, PAD)

    def kernel(g_ref, u_ref, d_ref, cat_ref, down_ref):
        i = pl.program_id(0)
        zero = jnp.zeros((pad - hid, width), jnp.bfloat16)
        cat_ref[hid:, :] = zero
        down_ref[hid:, :] = zero
        down_ref[:hid, :] = d_ref[0]

        @pl.when(i < n_exp)
        def _():
            cat_ref[:hid, :] = g_ref[0]

        @pl.when(i >= n_exp)
        def _():
            cat_ref[:hid, :] = u_ref[0]

    return pl.pallas_call(
        kernel,
        grid=(2 * n_exp,),
        out_shape=(
            jax.ShapeDtypeStruct((2 * n_exp * pad, width), jnp.bfloat16),
            jax.ShapeDtypeStruct((n_exp * pad, width), jnp.bfloat16),
        ),
        in_specs=[
            pl.BlockSpec((1, hid, width), lambda i: (jnp.minimum(i, n_exp - 1), 0, 0)),
            pl.BlockSpec((1, hid, width), lambda i: (jnp.maximum(i - n_exp, 0), 0, 0)),
            pl.BlockSpec((1, hid, width), lambda i: (i // 2, 0, 0)),
        ],
        out_specs=(
            pl.BlockSpec((pad, width), lambda i: (i, 0)),
            pl.BlockSpec((pad, width), lambda i: (i // 2, 0)),
        ),
        compiler_params=pltpu.CompilerParams(vmem_limit_bytes=14 * MIB),
        name="pack_weights",
    )(w_gate, w_up, w_down)


def forward(own, far, first, cat, down, width, n_exp, n_group, n_dp):
    half = sum(p.shape[1] for p in own)
    tall = 2 * half
    span = down.shape[0]
    pad = span // n_exp
    cols = width // n_dp
    bf = jnp.bfloat16
    f32 = jnp.float32
    nt = (((1,), (1,)), ((), ()))
    pieces = tuple(own) + tuple(far)
    block = 8 * n_group
    n_near = half // block

    def kernel(first_ref, *refs):
        rows = refs[: len(pieces)]
        cat_ref, down_ref, act_ref, near_ref, away_ref, cut_ref = refs[len(pieces) :]
        x = jnp.concatenate([r[0, :, :width] for r in rows], axis=0)
        y = jnp.concatenate([r[1, :, :width] for r in rows], axis=0)
        pre = lax.dot_general(x, cat_ref[...], nt, preferred_element_type=f32)
        back = lax.dot_general(y, down_ref[...], nt, preferred_element_type=f32)
        for d in range(n_dp):
            cut_ref[0, d] = x[:, d * cols : (d + 1) * cols]
            cut_ref[1, d] = y[:, d * cols : (d + 1) * cols]
        gate = pre[:, :span]
        up = pre[:, span:]
        tail = jnp.concatenate([r[0, :, width:] for r in rows], axis=0).astype(f32)
        lanes = lax.broadcasted_iota(jnp.int32, tail.shape, 1)
        quarter = tail.shape[1] // 4
        column = lax.broadcasted_iota(jnp.int32, gate.shape, 1)
        coef = jnp.zeros_like(gate)
        for e in range(n_exp):
            wanted = first_ref[0] + e
            hit = (lanes == wanted) | (lanes == wanted + quarter)
            mine = jnp.sum(jnp.where(hit, tail, 0.0), axis=1, keepdims=True)
            coef = jnp.where((column >= e * pad) & (column < (e + 1) * pad), mine, coef)
        sig = jax.nn.sigmoid(gate)
        silu = gate * sig
        back = back * coef
        act_ref[:, :span] = (back * up * sig * (1.0 + gate * (1.0 - sig))).astype(bf)
        act_ref[:, span : 2 * span] = (back * silu).astype(bf)
        act_ref[:, 2 * span :] = (coef * (silu * up)).astype(bf)
        part = jnp.dot(act_ref[:, : 2 * span], cat_ref[...], preferred_element_type=f32).astype(bf)
        for c, ref in enumerate((near_ref, away_ref)):
            for z in range(n_near):
                for g in range(n_group):
                    at = c * half + z * block + g * 8
                    ref[g, z] = part[at : at + 8]

    sums = jax.ShapeDtypeStruct((n_group, n_near, 8, width), bf)
    return pl.pallas_call(
        kernel,
        out_shape=(
            jax.ShapeDtypeStruct((tall, 3 * span), bf),
            sums,
            sums,
            jax.ShapeDtypeStruct((2, n_dp, tall, cols), bf),
        ),
        in_specs=[SMEM] + [VMEM] * (len(pieces) + 2),
        out_specs=(VMEM,) * 4,
        compiler_params=pltpu.CompilerParams(vmem_limit_bytes=12 * MIB),
        cost_estimate=pl.CostEstimate(
            flops=2 * tall * width * 5 * span, bytes_accessed=12 * MIB, transcendentals=tall * span
        ),
        name="forward",
    )(first, *pieces, cat, down)


def column_sums(place, offsets, n_dp, act_1, act_2, cut_1, cut_2, hid, n_exp, after=()):
    span = act_1.shape[1] // 3
    pad = span // n_exp
    cols = cut_1.shape[-1]
    tn = (((0,), (0,)), ((), ()))
    count = len(offsets)

    def kernel(place_ref, a_ref, b_ref, c_ref, d_ref, *rest):
        del place_ref
        outs, sums_ref = rest[len(after) : -1], rest[-1]
        act = jnp.concatenate([a_ref[...], b_ref[...]], axis=0)
        for kind in range(3):
            side = kind // 2
            x = jnp.concatenate([c_ref[side, 0], d_ref[side, 0]], axis=0)
            part = lax.dot_general(
                act[:, kind * span : (kind + 1) * span], x, tn, preferred_element_type=jnp.float32
            ).astype(jnp.bfloat16)
            for e in range(n_exp):
                sums_ref[e, :, kind * cols : (kind + 1) * cols] = part[e * pad : e * pad + hid, :]
        for step in range(count):

            @pl.when(pl.program_id(0) == step)
            def _(step=step):
                for e in range(n_exp):
                    outs[step * n_exp + e][...] = sums_ref[e]

    def picked(i, w):
        k = offsets[0]
        for step in range(1, count):
            k = jnp.where(i == step, offsets[step], k)
        return (0, lax.rem(w[0] + k, n_dp), 0, 0)

    fixed = lambda n: (lambda i, w: (0,) * n)
    outs = pl.pallas_call(
        kernel,
        out_shape=(jax.ShapeDtypeStruct((hid, 3 * cols), jnp.bfloat16),) * (n_exp * count),
        grid_spec=pltpu.PrefetchScalarGridSpec(
            num_scalar_prefetch=1,
            grid=(count,),
            in_specs=[
                pl.BlockSpec(act_1.shape, fixed(2)),
                pl.BlockSpec(act_2.shape, fixed(2)),
                pl.BlockSpec((2, 1) + cut_1.shape[2:], picked),
                pl.BlockSpec((2, 1) + cut_2.shape[2:], picked),
            ]
            + [pl.BlockSpec(memory_space=pl.ANY)] * len(after),
            out_specs=(VMEM,) * (n_exp * count),
            scratch_shapes=[pltpu.VMEM((n_exp, hid, 3 * cols), jnp.bfloat16)],
        ),
        compiler_params=pltpu.CompilerParams(vmem_limit_bytes=12 * MIB),
        cost_estimate=pl.CostEstimate(
            flops=2 * 512 * 3 * span * cols * count, bytes_accessed=4 * MIB * count, transcendentals=0
        ),
        name="column_sums",
    )(place, act_1, act_2, cut_1, cut_2, *after)
    return [outs[i * n_exp : (i + 1) * n_exp] for i in range(count)]


def finish(parts):
    n_exp = len(parts)
    hid, cols = parts[0][0].shape[0], parts[0][0].shape[1] // 3

    def kernel(*refs):
        outs = refs[-3:]
        for kind in range(3):
            span = slice(kind * cols, (kind + 1) * cols)
            at = 0
            for e in range(n_exp):
                mine = refs[at : at + len(parts[e])]
                at += len(parts[e])
                total = mine[0][:, span].astype(jnp.float32)
                for r in mine[1:]:
                    total = total + r[:, span].astype(jnp.float32)
                outs[kind][:, e, :] = total.astype(jnp.bfloat16)

    flat = [a for p in parts for a in p]
    outs = pl.pallas_call(
        kernel,
        grid=(1,),
        out_shape=(jax.ShapeDtypeStruct((hid, n_exp, cols), jnp.bfloat16),) * 3,
        in_specs=[VMEM] * len(flat),
        out_specs=(pl.BlockSpec((hid, n_exp, cols), lambda i: (0, 0, 0)),) * 3,
        compiler_params=pltpu.CompilerParams(vmem_limit_bytes=12 * MIB),
        name="finish",
    )(*flat)
    return tuple(o.transpose(1, 0, 2) for o in outs)


def small(kernel, out_shape, operands):
    return pl.pallas_call(
        kernel,
        out_shape=out_shape,
        in_specs=[VMEM] * len(operands),
        out_specs=jax.tree.map(lambda _: VMEM, out_shape),
        compiler_params=pltpu.CompilerParams(vmem_limit_bytes=4 * MIB),
    )(*operands)


def halves(lo, hi):
    lead, rows, width = lo.shape
    half = rows // 2

    def kernel(lo_ref, hi_ref, top_ref, bottom_ref):
        top_ref[...] = lo_ref[:, :half, :]
        bottom_ref[...] = hi_ref[:, half:, :]

    piece = jax.ShapeDtypeStruct((lead, half, width), lo.dtype)
    return small(kernel, (piece, piece), (lo, hi))


def add(a, b, after):
    def kernel(a_ref, b_ref, _, out_ref):
        wide = 4 * LANE
        steps = a.shape[1] // wide

        @pl.loop(0, steps)
        def _(i):
            span = pl.ds(pl.multiple_of(i * wide, wide), wide)
            out_ref[:, span] = (a_ref[:, span].astype(jnp.float32) + b_ref[:, span].astype(jnp.float32)).astype(a.dtype)

        rest = slice(steps * wide, a.shape[1])
        out_ref[:, rest] = (a_ref[:, rest].astype(jnp.float32) + b_ref[:, rest].astype(jnp.float32)).astype(a.dtype)

    return pl.pallas_call(
        kernel,
        out_shape=jax.ShapeDtypeStruct(a.shape, a.dtype),
        in_specs=[VMEM, VMEM, pl.BlockSpec(memory_space=pl.ANY)],
        out_specs=VMEM,
        compiler_params=pltpu.CompilerParams(vmem_limit_bytes=4 * MIB),
        name="add",
    )(a, b, after)


def merge_cores(near, arrived):
    n_group = near[0].shape[0]
    chips = sum(a.shape[1] for a in near)

    def kernel(*refs):
        outs = refs[4:]
        at = 0
        for a_ref, b_ref in zip(refs[:2], refs[2:4]):

            @pl.loop(0, a_ref.shape[1])
            def _(j, a_ref=a_ref, b_ref=b_ref, at=at):
                for k in range(n_group):
                    total = a_ref[k, j].astype(jnp.float32) + b_ref[k, j].astype(jnp.float32)
                    outs[k][at + j] = total.astype(jnp.bfloat16)

            at += a_ref.shape[1]

    one = jax.ShapeDtypeStruct((chips,) + near[0].shape[2:], near[0].dtype)
    return small(kernel, (one,) * n_group, (*near, *arrived))


def by_chip(parts):
    chips = parts[0].shape[0]
    half = chips // 2

    def kernel(*refs):
        outs = refs[len(parts) :]
        for j, offset in enumerate(OFFSETS):
            total = refs[0][j].astype(jnp.float32)
            for r in refs[1 : len(parts)]:
                total = total + r[j].astype(jnp.float32)
            ahead = offset % chips
            outs[ahead // half][ahead % half] = total.astype(jnp.bfloat16)

    one = jax.ShapeDtypeStruct((half,) + parts[0].shape[1:], parts[0].dtype)
    return small(kernel, (one, one), tuple(parts))


def fold(kept, arrived):
    half = kept.shape[0] // 2

    def kernel(a_ref, b_ref, *outs):
        for j in range(2 * half):
            total = a_ref[j].astype(jnp.float32) + b_ref[j].astype(jnp.float32)
            outs[j // half][j % half] = total.astype(jnp.bfloat16)

    one = jax.ShapeDtypeStruct((half,) + kept.shape[1:], kept.dtype)
    return small(kernel, (one, one), (kept, arrived))


def total_of(a, b):
    def kernel(a_ref, b_ref, out_ref):
        out_ref[...] = (a_ref[0].astype(jnp.float32) + b_ref[0].astype(jnp.float32)).astype(jnp.bfloat16)

    return small(kernel, jax.ShapeDtypeStruct(a.shape[1:], a.dtype), (a, b))


def shifted(x, axis, step):
    n = lax.axis_size(axis)
    return lax.ppermute(x, axis, [(i, (i - step) % n) for i in range(n)])


def partner(x):
    n = lax.axis_size("member")
    return lax.ppermute(x, "member", [(i, i ^ 1) for i in range(n)])


def step_of(tokens, cotangent, expert_ids, gate_weights, w_gate, w_up, w_down):
    n_group = lax.axis_size("group")
    n_dp = lax.axis_size("dp")
    n_exp, hid, width = w_gate.shape
    padded = up_to(width, LANE)
    place = lax.axis_index("dp").astype(jnp.int32).reshape(1)
    first = (lax.axis_index("group") * n_exp).astype(jnp.int32).reshape(1)
    mine = prepare(tokens, cotangent, expert_ids, gate_weights, padded)
    mine, place, first = lax.optimization_barrier((mine, place, first))
    own = join([mine] + [shifted(mine, "group", k) for k in range(1, n_group)])
    lo, hi, lo_far, hi_far = [own], [own], [], []
    own_far = partner(own)
    cat, down = pack_weights(w_gate, w_up, w_down)
    for step in range(3):
        lo.append(shifted(lo[-1], "member", -2))
        hi.append(shifted(hi[-1], "member", 2))
        if step == 0:
            lo[-1], hi[-1], cat, down = lax.optimization_barrier((lo[-1], hi[-1], cat, down))
        if step == 1:
            lo[-1], hi[-1], own_far, lo_far[0], hi_far[0] = lax.optimization_barrier(
                (lo[-1], hi[-1], own_far, lo_far[0], hi_far[0])
            )
        lo_far.append(partner(lo[-1]))
        hi_far.append(partner(hi[-1]))
    act_1, near_1, away_1, cut_1 = forward(
        [own, lo[1], hi[1], lo[2], hi[2]],
        [own_far, lo_far[0], hi_far[0], lo_far[1], hi_far[1]],
        first, cat, down, width, n_exp, n_group, n_dp,
    )
    top, bottom = halves(lo[3], hi[3])
    top = shifted(top, "member", -2)
    bottom = shifted(bottom, "member", 2)
    act_2, near_2, away_2, cut_2 = forward(
        [lo[3], hi[3], top, bottom],
        [lo_far[2], hi_far[2], partner(top), partner(bottom)],
        first, cat, down, width, n_exp, n_group, n_dp,
    )

    def shares(offsets, after=()):
        return column_sums(place, offsets, n_dp, act_1, act_2, cut_1, cut_2, hid, n_exp, after)

    ((far_0, far_1),) = shares((2,))
    right_0 = shifted(far_0, "dp", -1)
    left_1 = shifted(far_1, "dp", 1)
    away_1 = partner(away_1)
    away_2 = partner(away_2)
    both = merge_cores((near_1, near_2), (away_1, away_2))
    others = []
    for k in range(1, n_group):
        others.append(shifted(both[k], "group", -k))
    (next_0, next_1), (prev_0, prev_1), (here_0, here_1) = shares((1, 3, 0), (far_0,))
    from_left_1 = shifted(next_1, "dp", -1)
    from_right_0 = shifted(prev_0, "dp", 1)
    kept, sent = by_chip([both[0]] + others)
    sent = shifted(sent, "member", -8)
    joined_0 = add(next_0, right_0, kept)
    joined_1 = add(prev_1, left_1, kept)
    from_left_0 = shifted(joined_0, "dp", -1)
    from_right_1 = shifted(joined_1, "dp", 1)
    kept, sent = fold(kept, sent)
    kept, sent = fold(kept, shifted(sent, "member", -4))
    grad_tokens = total_of(kept, shifted(sent, "member", -2))
    grads = finish([[here_0, from_right_0, from_left_0], [here_1, from_left_1, from_right_1]])
    return (grad_tokens,) + tuple(grads)


def solution(mesh):
    placed = P(("dp", "group", "member"), None)
    weight = P("group", "member", None)
    grad = P("group", "member", "dp")
    return jax.shard_map(
        step_of,
        mesh=mesh,
        in_specs=(placed, placed, placed, placed, weight, weight, weight),
        out_specs=(placed, grad, grad, grad),
        check_vma=False,
    )
```

```python
import jax
import jax.numpy as jnp
from jax import lax
from jax.experimental import pallas as pl
from jax.experimental.pallas import tpu as pltpu
from jax.sharding import PartitionSpec as P


LANE = 128
PAD = 64
MIB = 1 << 20
OFFSETS = (0, -1, 1, -2, 2, -3, 3, 4)
VMEM = pl.BlockSpec(memory_space=pltpu.VMEM)
SMEM = pl.BlockSpec(memory_space=pltpu.SMEM)


def up_to(n, k):
    return -(-n // k) * k


def prepare(tokens, cotangent, expert_ids, gate_weights, padded):
    rows, width = tokens.shape
    room = padded - width
    quarter = room // 4
    bf = jnp.bfloat16

    def kernel(*refs):
        out_ref, sems = refs[4], refs[9]
        copies = [pltpu.make_async_copy(refs[i], refs[5 + i], sems.at[i]) for i in range(4)]
        for copy in copies:
            copy.start()
        for copy in copies:
            copy.wait()
        tok_ref, cot_ref, id_ref, weight_ref = refs[5:9]
        lane = lax.broadcasted_iota(jnp.int32, (rows, room), 1)
        expert = jnp.where(lane < quarter, lane, lane - quarter)
        diagonal = lax.broadcasted_iota(jnp.int32, (rows, rows), 0) == lax.broadcasted_iota(jnp.int32, (rows, rows), 1)
        coef = jnp.zeros((rows, room), jnp.float32)
        for k in range(id_ref.shape[0]):
            ids = jnp.sum(jnp.where(diagonal, id_ref[k : k + 1, :], 0), axis=1, keepdims=True)
            weights = jnp.sum(jnp.where(diagonal, weight_ref[k : k + 1, :], 0.0), axis=1, keepdims=True)
            coef = coef + jnp.where(ids == expert, weights, 0.0)
        high = coef.astype(bf).astype(jnp.float32)
        tail = jnp.where(lane < quarter, high, jnp.where(lane < 2 * quarter, coef - high, 0.0))
        out_ref[0, :, :width] = tok_ref[...]
        out_ref[0, :, width:] = tail.astype(bf)
        out_ref[1, :, :width] = cot_ref[...]
        out_ref[1, :, width:] = jnp.zeros((rows, room), bf)

    operands = (tokens, cotangent, expert_ids.T, gate_weights.T)
    return pl.pallas_call(
        kernel,
        out_shape=jax.ShapeDtypeStruct((2, rows, padded), bf),
        in_specs=[pl.BlockSpec(memory_space=pltpu.HBM)] * 4,
        out_specs=VMEM,
        scratch_shapes=[pltpu.VMEM(x.shape, x.dtype) for x in operands] + [pltpu.SemaphoreType.DMA((4,))],
        name="prepare",
    )(*operands)


def join(pieces):
    lead, rows, width = pieces[0].shape

    def kernel(*refs):
        for i, ref in enumerate(refs[:-1]):
            refs[-1][:, i * rows : (i + 1) * rows, :] = ref[...]

    return pl.pallas_call(
        kernel,
        out_shape=jax.ShapeDtypeStruct((lead, rows * len(pieces), width), pieces[0].dtype),
        compiler_params=pltpu.CompilerParams(vmem_limit_bytes=4 * MIB),
        name="join",
    )(*pieces)


def pack_weights(w_gate, w_up, w_down):
    n_exp, hid, width = w_gate.shape
    pad = up_to(hid, PAD)

    def kernel(g_ref, u_ref, d_ref, cat_ref, down_ref):
        i = pl.program_id(0)
        zero = jnp.zeros((pad - hid, width), jnp.bfloat16)
        cat_ref[hid:, :] = zero
        down_ref[hid:, :] = zero
        down_ref[:hid, :] = d_ref[0]

        @pl.when(i < n_exp)
        def _():
            cat_ref[:hid, :] = g_ref[0]

        @pl.when(i >= n_exp)
        def _():
            cat_ref[:hid, :] = u_ref[0]

    return pl.pallas_call(
        kernel,
        grid=(2 * n_exp,),
        out_shape=(
            jax.ShapeDtypeStruct((2 * n_exp * pad, width), jnp.bfloat16),
            jax.ShapeDtypeStruct((n_exp * pad, width), jnp.bfloat16),
        ),
        in_specs=[
            pl.BlockSpec((1, hid, width), lambda i: (jnp.minimum(i, n_exp - 1), 0, 0)),
            pl.BlockSpec((1, hid, width), lambda i: (jnp.maximum(i - n_exp, 0), 0, 0)),
            pl.BlockSpec((1, hid, width), lambda i: (i // 2, 0, 0)),
        ],
        out_specs=(
            pl.BlockSpec((pad, width), lambda i: (i, 0)),
            pl.BlockSpec((pad, width), lambda i: (i // 2, 0)),
        ),
        compiler_params=pltpu.CompilerParams(vmem_limit_bytes=14 * MIB),
        name="pack_weights",
    )(w_gate, w_up, w_down)


def put_shares(act_ref, cat_ref, outs):
    span = act_ref.shape[1] // 3
    part = jnp.dot(act_ref[:, : 2 * span], cat_ref[...], preferred_element_type=jnp.float32).astype(jnp.bfloat16)
    n_group, n_near, rows, _ = outs[0].shape
    at = 0
    for ref in outs:
        for z in range(n_near):
            for g in range(n_group):
                ref[g, z] = part[at : at + rows]
                at += rows


def token_shares(act, cat, n_group, after):
    width = cat.shape[1]

    def kernel(act_ref, cat_ref, _, *outs):
        put_shares(act_ref, cat_ref, outs)

    sums = jax.ShapeDtypeStruct((n_group, act.shape[0] // (16 * n_group), 8, width), jnp.bfloat16)
    return pl.pallas_call(
        kernel,
        out_shape=(sums, sums),
        in_specs=[VMEM, VMEM, pl.BlockSpec(memory_space=pl.ANY)],
        out_specs=(VMEM, VMEM),
        compiler_params=pltpu.CompilerParams(vmem_limit_bytes=12 * MIB),
        name="token_shares",
    )(act, cat, after)


def forward(own, far, first, cat, down, width, n_exp, n_group, n_dp, shares=True):
    half = sum(p.shape[1] for p in own)
    tall = 2 * half
    span = down.shape[0]
    pad = span // n_exp
    cols = width // n_dp
    bf = jnp.bfloat16
    f32 = jnp.float32
    nt = (((1,), (1,)), ((), ()))
    pieces = tuple(own) + tuple(far)
    block = 8 * n_group
    n_near = half // block

    def kernel(first_ref, *refs):
        rows = refs[: len(pieces)]
        cat_ref, down_ref = refs[len(pieces) : len(pieces) + 2]
        act_ref, cut_ref = refs[len(pieces) + 2], refs[-1]
        x = jnp.concatenate([r[0, :, :width] for r in rows], axis=0)
        y = jnp.concatenate([r[1, :, :width] for r in rows], axis=0)
        pre = lax.dot_general(x, cat_ref[...], nt, preferred_element_type=f32)
        back = lax.dot_general(y, down_ref[...], nt, preferred_element_type=f32)
        for d in range(n_dp):
            cut_ref[0, d] = x[:, d * cols : (d + 1) * cols]
            cut_ref[1, d] = y[:, d * cols : (d + 1) * cols]
        gate = pre[:, :span]
        up = pre[:, span:]
        tail = jnp.concatenate([r[0, :, width:] for r in rows], axis=0).astype(f32)
        lanes = lax.broadcasted_iota(jnp.int32, tail.shape, 1)
        quarter = tail.shape[1] // 4
        column = lax.broadcasted_iota(jnp.int32, gate.shape, 1)
        coef = jnp.zeros_like(gate)
        for e in range(n_exp):
            wanted = first_ref[0] + e
            hit = (lanes == wanted) | (lanes == wanted + quarter)
            mine = jnp.sum(jnp.where(hit, tail, 0.0), axis=1, keepdims=True)
            coef = jnp.where((column >= e * pad) & (column < (e + 1) * pad), mine, coef)
        sig = jax.nn.sigmoid(gate)
        silu = gate * sig
        back = back * coef
        act_ref[:, :span] = (back * up * sig * (1.0 + gate * (1.0 - sig))).astype(bf)
        act_ref[:, span : 2 * span] = (back * silu).astype(bf)
        act_ref[:, 2 * span :] = (coef * (silu * up)).astype(bf)
        if shares:
            put_shares(act_ref, cat_ref, refs[-3:-1])

    sums = (jax.ShapeDtypeStruct((n_group, n_near, 8, width), bf),) * (2 * shares)
    return pl.pallas_call(
        kernel,
        out_shape=(
            jax.ShapeDtypeStruct((tall, 3 * span), bf),
            *sums,
            jax.ShapeDtypeStruct((2, n_dp, tall, cols), bf),
        ),
        in_specs=[SMEM] + [VMEM] * (len(pieces) + 2),
        out_specs=(VMEM,) * (2 + len(sums)),
        compiler_params=pltpu.CompilerParams(vmem_limit_bytes=12 * MIB),
        cost_estimate=pl.CostEstimate(
            flops=2 * tall * width * 5 * span, bytes_accessed=12 * MIB, transcendentals=tall * span
        ),
        name="forward",
    )(first, *pieces, cat, down)


def column_sums(place, offsets, n_dp, act_1, act_2, cut_1, cut_2, hid, n_exp, after=()):
    span = act_1.shape[1] // 3
    pad = span // n_exp
    cols = cut_1.shape[-1]
    tn = (((0,), (0,)), ((), ()))
    count = len(offsets)

    def kernel(place_ref, a_ref, b_ref, c_ref, d_ref, *rest):
        del place_ref
        outs, sums_ref = rest[len(after) : -1], rest[-1]
        act = jnp.concatenate([a_ref[...], b_ref[...]], axis=0)
        for kind in range(3):
            side = kind // 2
            x = jnp.concatenate([c_ref[side, 0], d_ref[side, 0]], axis=0)
            part = lax.dot_general(
                act[:, kind * span : (kind + 1) * span], x, tn, preferred_element_type=jnp.float32
            ).astype(jnp.bfloat16)
            for e in range(n_exp):
                sums_ref[e, :, kind * cols : (kind + 1) * cols] = part[e * pad : e * pad + hid, :]
        for step in range(count):

            @pl.when(pl.program_id(0) == step)
            def _(step=step):
                for e in range(n_exp):
                    outs[step * n_exp + e][...] = sums_ref[e]

    def picked(i, w):
        k = offsets[0]
        for step in range(1, count):
            k = jnp.where(i == step, offsets[step], k)
        return (0, lax.rem(w[0] + k, n_dp), 0, 0)

    fixed = lambda n: (lambda i, w: (0,) * n)
    outs = pl.pallas_call(
        kernel,
        out_shape=(jax.ShapeDtypeStruct((hid, 3 * cols), jnp.bfloat16),) * (n_exp * count),
        grid_spec=pltpu.PrefetchScalarGridSpec(
            num_scalar_prefetch=1,
            grid=(count,),
            in_specs=[
                pl.BlockSpec(act_1.shape, fixed(2)),
                pl.BlockSpec(act_2.shape, fixed(2)),
                pl.BlockSpec((2, 1) + cut_1.shape[2:], picked),
                pl.BlockSpec((2, 1) + cut_2.shape[2:], picked),
            ]
            + [pl.BlockSpec(memory_space=pl.ANY)] * len(after),
            out_specs=(VMEM,) * (n_exp * count),
            scratch_shapes=[pltpu.VMEM((n_exp, hid, 3 * cols), jnp.bfloat16)],
        ),
        compiler_params=pltpu.CompilerParams(vmem_limit_bytes=12 * MIB),
        cost_estimate=pl.CostEstimate(
            flops=2 * 512 * 3 * span * cols * count, bytes_accessed=4 * MIB * count, transcendentals=0
        ),
        name="column_sums",
    )(place, act_1, act_2, cut_1, cut_2, *after)
    return [outs[i * n_exp : (i + 1) * n_exp] for i in range(count)]


def finish(parts):
    n_exp = len(parts)
    hid, cols = parts[0][0].shape[0], parts[0][0].shape[1] // 3

    def kernel(*refs):
        outs = refs[-3:]
        for kind in range(3):
            span = slice(kind * cols, (kind + 1) * cols)
            at = 0
            for e in range(n_exp):
                mine = refs[at : at + len(parts[e])]
                at += len(parts[e])
                total = mine[0][:, span].astype(jnp.float32)
                for r in mine[1:]:
                    total = total + r[:, span].astype(jnp.float32)
                outs[kind][:, e, :] = total.astype(jnp.bfloat16)

    flat = [a for p in parts for a in p]
    outs = pl.pallas_call(
        kernel,
        grid=(1,),
        out_shape=(jax.ShapeDtypeStruct((hid, n_exp, cols), jnp.bfloat16),) * 3,
        in_specs=[VMEM] * len(flat),
        out_specs=(pl.BlockSpec((hid, n_exp, cols), lambda i: (0, 0, 0)),) * 3,
        compiler_params=pltpu.CompilerParams(vmem_limit_bytes=12 * MIB),
        name="finish",
    )(*flat)
    return tuple(o.transpose(1, 0, 2) for o in outs)


def small(kernel, out_shape, operands):
    return pl.pallas_call(
        kernel,
        out_shape=out_shape,
        in_specs=[VMEM] * len(operands),
        out_specs=jax.tree.map(lambda _: VMEM, out_shape),
        compiler_params=pltpu.CompilerParams(vmem_limit_bytes=4 * MIB),
    )(*operands)


def halves(lo, hi):
    lead, rows, width = lo.shape
    half = rows // 2

    def kernel(lo_ref, hi_ref, top_ref, bottom_ref):
        top_ref[...] = lo_ref[:, :half, :]
        bottom_ref[...] = hi_ref[:, half:, :]

    piece = jax.ShapeDtypeStruct((lead, half, width), lo.dtype)
    return small(kernel, (piece, piece), (lo, hi))


def add(a, b, after):
    def kernel(a_ref, b_ref, _, out_ref):
        wide = 4 * LANE
        steps = a.shape[1] // wide

        @pl.loop(0, steps)
        def _(i):
            span = pl.ds(pl.multiple_of(i * wide, wide), wide)
            out_ref[:, span] = (a_ref[:, span].astype(jnp.float32) + b_ref[:, span].astype(jnp.float32)).astype(a.dtype)

        rest = slice(steps * wide, a.shape[1])
        out_ref[:, rest] = (a_ref[:, rest].astype(jnp.float32) + b_ref[:, rest].astype(jnp.float32)).astype(a.dtype)

    return pl.pallas_call(
        kernel,
        out_shape=jax.ShapeDtypeStruct(a.shape, a.dtype),
        in_specs=[VMEM, VMEM, pl.BlockSpec(memory_space=pl.ANY)],
        out_specs=VMEM,
        compiler_params=pltpu.CompilerParams(vmem_limit_bytes=4 * MIB),
        name="add",
    )(a, b, after)


def merge_cores(near, arrived):
    n_group = near[0].shape[0]
    chips = sum(a.shape[1] for a in near)

    def kernel(*refs):
        outs = refs[4:]
        at = 0
        for a_ref, b_ref in zip(refs[:2], refs[2:4]):

            @pl.loop(0, a_ref.shape[1])
            def _(j, a_ref=a_ref, b_ref=b_ref, at=at):
                for k in range(n_group):
                    total = a_ref[k, j].astype(jnp.float32) + b_ref[k, j].astype(jnp.float32)
                    outs[k][at + j] = total.astype(jnp.bfloat16)

            at += a_ref.shape[1]

    one = jax.ShapeDtypeStruct((chips,) + near[0].shape[2:], near[0].dtype)
    return small(kernel, (one,) * n_group, (*near, *arrived))


def by_chip(parts):
    chips = parts[0].shape[0]
    half = chips // 2

    def kernel(*refs):
        outs = refs[len(parts) :]
        for j, offset in enumerate(OFFSETS):
            total = refs[0][j].astype(jnp.float32)
            for r in refs[1 : len(parts)]:
                total = total + r[j].astype(jnp.float32)
            ahead = offset % chips
            outs[ahead % 2][ahead // 2] = total.astype(jnp.bfloat16)

    one = jax.ShapeDtypeStruct((half,) + parts[0].shape[1:], parts[0].dtype)
    return small(kernel, (one, one), tuple(parts))


def fold(kept, arrived):
    half = kept.shape[0] // 2

    def kernel(a_ref, b_ref, *outs):
        for j in range(2 * half):
            total = a_ref[j].astype(jnp.float32) + b_ref[j].astype(jnp.float32)
            outs[j % 2][j // 2] = total.astype(jnp.bfloat16)

    one = jax.ShapeDtypeStruct((half,) + kept.shape[1:], kept.dtype)
    return small(kernel, (one, one), (kept, arrived))


def total_of(a, b):
    def kernel(a_ref, b_ref, out_ref):
        out_ref[...] = (a_ref[0].astype(jnp.float32) + b_ref[0].astype(jnp.float32)).astype(jnp.bfloat16)

    return small(kernel, jax.ShapeDtypeStruct(a.shape[1:], a.dtype), (a, b))


def shifted(x, axis, step):
    n = lax.axis_size(axis)
    return lax.ppermute(x, axis, [(i, (i - step) % n) for i in range(n)])


def partner(x):
    n = lax.axis_size("member")
    return lax.ppermute(x, "member", [(i, i ^ 1) for i in range(n)])


def step_of(tokens, cotangent, expert_ids, gate_weights, w_gate, w_up, w_down):
    n_group = lax.axis_size("group")
    n_dp = lax.axis_size("dp")
    n_exp, hid, width = w_gate.shape
    padded = up_to(width, LANE)
    place = lax.axis_index("dp").astype(jnp.int32).reshape(1)
    first = (lax.axis_index("group") * n_exp).astype(jnp.int32).reshape(1)
    mine = prepare(tokens, cotangent, expert_ids, gate_weights, padded)
    mine, place, first = lax.optimization_barrier((mine, place, first))
    own = join([mine] + [shifted(mine, "group", k) for k in range(1, n_group)])
    lo, hi, lo_far, hi_far = [own], [own], [], []
    own_far = partner(own)
    cat, down = pack_weights(w_gate, w_up, w_down)
    for step in range(3):
        lo.append(shifted(lo[-1], "member", -2))
        hi.append(shifted(hi[-1], "member", 2))
        if step == 0:
            lo[-1], hi[-1], cat, down = lax.optimization_barrier((lo[-1], hi[-1], cat, down))
        if step == 1:
            lo[-1], hi[-1], own_far, lo_far[0], hi_far[0] = lax.optimization_barrier(
                (lo[-1], hi[-1], own_far, lo_far[0], hi_far[0])
            )
        lo_far.append(partner(lo[-1]))
        hi_far.append(partner(hi[-1]))
    act_1, near_1, away_1, cut_1 = forward(
        [own, lo[1], hi[1], lo[2], hi[2]],
        [own_far, lo_far[0], hi_far[0], lo_far[1], hi_far[1]],
        first, cat, down, width, n_exp, n_group, n_dp,
    )
    top, bottom = halves(lo[3], hi[3])
    top = shifted(top, "member", -2)
    bottom = shifted(bottom, "member", 2)
    act_2, cut_2 = forward(
        [lo[3], hi[3], top, bottom],
        [lo_far[2], hi_far[2], partner(top), partner(bottom)],
        first, cat, down, width, n_exp, n_group, n_dp, shares=False,
    )

    def shares(offsets, after=()):
        return column_sums(place, offsets, n_dp, act_1, act_2, cut_1, cut_2, hid, n_exp, after)

    ((far_0, far_1),) = shares((2,))
    right_0 = shifted(far_0, "dp", -1)
    left_1 = shifted(far_1, "dp", 1)
    near_2, away_2 = token_shares(act_2, cat, n_group, far_0)
    away_1 = partner(away_1)
    away_2 = partner(away_2)
    both = merge_cores((near_1, near_2), (away_1, away_2))
    others = []
    for k in range(1, n_group):
        others.append(shifted(both[k], "group", -k))
    (next_0, next_1), (prev_0, prev_1), (here_0, here_1) = shares((1, 3, 0), (far_0,))
    from_left_1 = shifted(next_1, "dp", -1)
    from_right_0 = shifted(prev_0, "dp", 1)
    kept, sent = by_chip([both[0]] + others)
    sent = shifted(sent, "member", -2)
    joined_0 = add(next_0, right_0, kept)
    joined_1 = add(prev_1, left_1, kept)
    from_left_0 = shifted(joined_0, "dp", -1)
    from_right_1 = shifted(joined_1, "dp", 1)
    kept, sent = fold(kept, sent)
    kept, sent = fold(kept, shifted(sent, "member", -4))
    grad_tokens = total_of(kept, shifted(sent, "member", -8))
    grads = finish([[here_0, from_right_0, from_left_0], [here_1, from_left_1, from_right_1]])
    return (grad_tokens,) + tuple(grads)


def solution(mesh):
    placed = P(("dp", "group", "member"), None)
    weight = P("group", "member", None)
    grad = P("group", "member", "dp")
    return jax.shard_map(
        step_of,
        mesh=mesh,
        in_specs=(placed, placed, placed, placed, weight, weight, weight),
        out_specs=(placed, grad, grad, grad),
        check_vma=False,
    )
```
